128 devices in a mesh: row: 8 (over z_lo, x), col: 16 (over y, z_hi, core).
Axes of the slice: x: 4, y: 4, z: 4 (z_hi: 2, z_lo: 2; z = z_hi * 2 + z_lo), core: 2. Of those that a mesh axis runs over, the one named last changes fastest.
Arguments:
- theta_one: bfloat16 [8192, 4096], P('row', 'col'), may hold values from -4 to 4
- theta_two: bfloat16 [4096, 32768], P('row', 'col'), may hold values from -4 to 4
- cost_one: bfloat16 [8192, 4096], P('row', 'col'), may hold values from -3 to 3
- cost_two: bfloat16 [4096, 32768], P('row', 'col'), may hold values from -3 to 3
- depot_price: float32 [8192], P('row'), may hold values from 0.5 to 2
- hub_price: float32 [4096], replicated, may hold values from -3 to 3
- zone_price: float32 [32768], P('col'), may hold values from 0.5 to 2
- mask_one: int32 [64, 32], P('row', 'col'), may hold values 0 or 1
- mask_two: int32 [32, 256], P('row', 'col'), may hold values 0 or 1
- supply: int32 [8192], P('row'), may hold values from 1 to 4
- demand: int32 [32768], P('col'), may hold values from 1 to 4
- capacity: int32 [4096], replicated, may hold values from 1 to 8
- cot_flow_one: bfloat16 [8192, 4096], P('row', 'col'), may hold values from -6 to 6
- cot_flow_two: bfloat16 [4096, 32768], P('row', 'col'), may hold values from -6 to 6
- cot_depot: float32 [8192], P('row'), may hold values from -6 to 6
- cot_hub: float32 [4096], replicated, may hold values from -6 to 6
- cot_zone: float32 [32768], P('col'), may hold values from -6 to 6
Outputs:
- grad_theta_one: float32 [8192, 4096], P('row', 'col')
- grad_theta_two: float32 [4096, 32768], P('row', 'col')
- grad_cost_one: float32 [8192, 4096], P('row', 'col')
- grad_cost_two: float32 [4096, 32768], P('row', 'col')
- grad_depot: float32 [8192], P('row')
- grad_hub: float32 [4096], replicated
- grad_zone: float32 [32768], P('col')
The draws below stay inside these ranges and needn't reach their ends.
All inputs are finite; a program needn't handle non-finite values. No bound on the sum of `mask_one` or of `mask_two` on one device may be relied on, other than what follows from the above.
Results may differ from the reference program's by a relative error of at most 0.0003.
Values sent between devices are 32-bit elements; how exact they have to be, the bound alone decides.
A program may use at most 64 MiB of HBM per device.

```python
import math
import jax
import jax.numpy as jnp

DEP = 8192
HUB = 4096
ZONE = 32768
TILE = 128
ITERS = 2


def set_ends(array, own_key, least, high):
    place = [jax.random.randint(jax.random.fold_in(own_key, axis), (), 0, length) for axis, length in enumerate(array.shape)]
    longest = array.shape.index(max(array.shape))
    next_to = place[:longest] + [(place[longest] + 1) % array.shape[longest]] + place[longest + 1:]
    return array.at[tuple(place)].set(least).at[tuple(next_to)].set(high)


def steps_of(stream_key, shape, split, smallest, high):
    loudness = 1.0
    for position, shards_of in split:
        draws = jax.random.uniform(jax.random.fold_in(jax.random.fold_in(stream_key, 6), position), (shards_of,), jnp.float32, smallest / len(split), high / len(split))
        loudness = loudness * jnp.repeat(jnp.exp(draws), shape[position] // shards_of).reshape((-1,) + (1,) * (len(shape) - 1 - position))
    return loudness


def normal_values(own_key, extent, scale, bound, cuts=(), dtype=jnp.bfloat16):
    loudness = steps_of(own_key, extent, cuts, -0.22, 0.18) if cuts else 1.0
    values = jax.random.normal(own_key, extent, jnp.float32) * scale * loudness
    return jnp.minimum(jnp.maximum(values, -bound), bound).astype(dtype)


def setup_inputs(seed: int = 0) -> dict:
    arg_keys = jax.random.split(jax.random.key(seed), 18)
    theta_one = normal_values(arg_keys[0], (DEP, HUB), 1.0, 4.0, ((0, 8), (1, 16)))
    theta_two = normal_values(arg_keys[1], (HUB, ZONE), 1.0, 4.0, ((0, 8), (1, 16)))
    cost_one = normal_values(arg_keys[2], (DEP, HUB), 0.5, 3.0, ((0, 8), (1, 16)))
    cost_two = normal_values(arg_keys[3], (HUB, ZONE), 0.5, 3.0, ((0, 8), (1, 16)))
    depot_price = jnp.clip(jnp.exp(math.log(2.0) - 1.3862944 * jax.random.uniform(arg_keys[4], (DEP,), jnp.float32) ** steps_of(arg_keys[4], (DEP,), ((0, 8),), -0.2, 0.2)), 0.5, 2.0)
    hub_price = normal_values(arg_keys[5], (HUB,), 0.5, 3.0, (), jnp.float32)
    zone_price = jnp.clip(jnp.exp(math.log(2.0) - 1.3862944 * jax.random.uniform(arg_keys[6], (ZONE,), jnp.float32) ** steps_of(arg_keys[6], (ZONE,), ((0, 16),), -0.2, 0.2)), 0.5, 2.0)
    mask_one = set_ends((jax.random.randint(arg_keys[7], (DEP // TILE, HUB // TILE), 0, 3) < 2).astype(jnp.int32), jax.random.fold_in(arg_keys[7], 1), 0, 1)
    mask_two = set_ends((jax.random.randint(arg_keys[8], (HUB // TILE, ZONE // TILE), 0, 3) < 2).astype(jnp.int32), jax.random.fold_in(arg_keys[8], 1), 0, 1)
    supply = set_ends(jax.random.randint(arg_keys[9], (DEP,), 1, 5), jax.random.fold_in(arg_keys[9], 1), 1, 4).astype(jnp.int32)
    demand = set_ends(jax.random.randint(arg_keys[10], (ZONE,), 1, 5), jax.random.fold_in(arg_keys[10], 1), 1, 4).astype(jnp.int32)
    capacity = set_ends(jax.random.randint(arg_keys[11], (HUB,), 1, 9), jax.random.fold_in(arg_keys[11], 1), 1, 8).astype(jnp.int32)
    cot_flow_one = normal_values(arg_keys[12], (DEP, HUB), 1.0, 6.0, ((0, 8), (1, 16)))
    cot_flow_two = normal_values(arg_keys[13], (HUB, ZONE), 1.0, 6.0, ((0, 8), (1, 16)))
    cot_depot = normal_values(arg_keys[14], (DEP,), 1.0, 6.0, ((0, 8),), jnp.float32)
    cot_hub = normal_values(arg_keys[15], (HUB,), 1.0, 6.0, (), jnp.float32)
    cot_zone = normal_values(arg_keys[16], (ZONE,), 1.0, 6.0, ((0, 16),), jnp.float32)
    return {"theta_one": theta_one, "theta_two": theta_two, "cost_one": cost_one, "cost_two": cost_two, "depot_price": depot_price, "hub_price": hub_price, "zone_price": zone_price, "mask_one": mask_one, "mask_two": mask_two, "supply": supply, "demand": demand, "capacity": capacity, "cot_flow_one": cot_flow_one, "cot_flow_two": cot_flow_two, "cot_depot": cot_depot, "cot_hub": cot_hub, "cot_zone": cot_zone}


STEP_PRIMAL = 0.5
STEP_DUAL = 0.5
HUB_RATE = 4.0


def expand(tiles, tile_size):
    block_rows, block_cols = tiles.shape
    spread = jnp.broadcast_to(tiles.astype(jnp.float32)[:, None, :, None], (block_rows, tile_size, block_cols, tile_size))
    return spread.reshape(block_rows * tile_size, block_cols * tile_size)


def logistic(values):
    return 1.0 / (1.0 + jnp.exp(-values))


def slope(values):
    sigma = logistic(values)
    return sigma * (1.0 - sigma)


def reference(theta_one, theta_two, cost_one, cost_two, depot_price, hub_price, zone_price, mask_one, mask_two, supply, demand, capacity, cot_flow_one, cot_flow_two, cot_depot, cot_hub, cot_zone):
    levels = capacity.astype(jnp.float32)
    keep_one = expand(mask_one, TILE) * levels[None, :]
    keep_two = expand(mask_two, TILE) * (0.25 * levels)[:, None]
    supply_level = 0.5 * supply.astype(jnp.float32)
    demand_level = 0.125 * demand.astype(jnp.float32)
    cost_first = cost_one.astype(jnp.float32)
    cost_second = cost_two.astype(jnp.float32)
    states_one = [theta_one.astype(jnp.float32)]
    states_two = [theta_two.astype(jnp.float32)]
    depot_now, hub_now, zone_now = depot_price, hub_price, zone_price
    depot_saved, zone_saved, depot_grow, zone_grow = [], [], [], []
    for counter in range(ITERS):
        old_one = states_one[-1]
        old_two = states_two[-1]
        next_one = old_one - STEP_PRIMAL * (cost_first + depot_now[:, None] + hub_now[None, :])
        next_two = old_two - STEP_PRIMAL * (cost_second - hub_now[:, None] - zone_now[None, :])
        bar_one = keep_one * (2.0 * logistic(next_one) - logistic(old_one))
        bar_two = keep_two * (2.0 * logistic(next_two) - logistic(old_two))
        growth_depot = jnp.exp(STEP_DUAL * (jnp.sum(bar_one, axis=1) / HUB - supply_level))
        growth_zone = jnp.exp(STEP_DUAL * (demand_level - jnp.sum(bar_two, axis=0) / HUB))
        depot_now = depot_now * growth_depot
        zone_now = zone_now * growth_zone
        hub_now = hub_now + HUB_RATE * (jnp.sum(bar_one, axis=0) - jnp.sum(bar_two, axis=1)) / DEP
        depot_saved.append(depot_now)
        zone_saved.append(zone_now)
        depot_grow.append(growth_depot)
        zone_grow.append(growth_zone)
        states_one.append(next_one)
        states_two.append(next_two)
    adj_one = cot_flow_one.astype(jnp.float32) * keep_one * slope(states_one[-1])
    adj_two = cot_flow_two.astype(jnp.float32) * keep_two * slope(states_two[-1])
    adj_depot, adj_hub, adj_zone = cot_depot, cot_hub, cot_zone
    grad_first = jnp.zeros_like(adj_one)
    grad_second = jnp.zeros_like(adj_two)
    for counter in range(ITERS - 1, -1, -1):
        push_depot = adj_depot * depot_saved[counter] * (STEP_DUAL / HUB)
        push_zone = -adj_zone * zone_saved[counter] * (STEP_DUAL / HUB)
        push_hub = adj_hub * (HUB_RATE / DEP)
        weight_one = push_depot[:, None] + push_hub[None, :]
        weight_two = push_zone[None, :] - push_hub[:, None]
        total_one = adj_one + 2.0 * weight_one * keep_one * slope(states_one[counter + 1])
        total_two = adj_two + 2.0 * weight_two * keep_two * slope(states_two[counter + 1])
        adj_one = total_one - weight_one * keep_one * slope(states_one[counter])
        adj_two = total_two - weight_two * keep_two * slope(states_two[counter])
        grad_first = grad_first - STEP_PRIMAL * total_one
        grad_second = grad_second - STEP_PRIMAL * total_two
        adj_depot = adj_depot * depot_grow[counter] - STEP_PRIMAL * jnp.sum(total_one, axis=1)
        adj_hub = adj_hub + STEP_PRIMAL * (jnp.sum(total_two, axis=1) - jnp.sum(total_one, axis=0))
        adj_zone = adj_zone * zone_grow[counter] + STEP_PRIMAL * jnp.sum(total_two, axis=0)
    return (adj_one, adj_two, grad_first, grad_second, adj_depot, adj_hub, adj_zone)
```

```python
import functools

import jax
import jax.numpy as jnp
from jax import lax
from jax.experimental import pallas as pl
from jax.experimental.pallas import tpu as pltpu
from jax.sharding import PartitionSpec as P

DEP = 8192
HUB = 4096
TILE = 128
LANES = 128
STEP = 0.5
HUB_RATE = 4.0
CHUNK = 64
MESH = pl.DeviceIdType.MESH
F32 = jnp.float32


def fold(values):
    return jnp.sum(values.reshape(values.shape[0] // 8, 8, LANES), axis=0)


def spread(row):
    return jnp.transpose(jnp.broadcast_to(row, (LANES, LANES)))


def kernel(
    n_row,
    n_col,
    theta_one,
    theta_two,
    cost_one,
    cost_two,
    depot_hbm,
    hub_hbm,
    zone_hbm,
    mask_one,
    mask_two,
    supply_hbm,
    demand_hbm,
    capacity_hbm,
    cot_one,
    cot_two,
    cot_depot_hbm,
    cot_hub_hbm,
    cot_zone_hbm,
    grad_one,
    grad_two,
    grad_cost_one,
    grad_cost_two,
    grad_depot,
    grad_hub,
    grad_zone,
    th1,
    th2,
    co1,
    co2,
    ct1,
    ct2,
    depot,
    hub,
    zone,
    supply,
    demand,
    capacity,
    cot_depot,
    cot_hub,
    cot_zone,
    a1,
    a2,
    b1,
    b2,
    side_depot,
    side_hub,
    side_cap,
    stage_depot,
    stage_hub,
    stage_zone,
    send_d,
    send_z,
    send_h1,
    send_h2,
    got_d,
    got_z,
    got_h1,
    got_h2,
    got_g,
    load_sem,
    small_sem,
    d_out,
    d_in,
    z_out,
    z_in,
    h1_out,
    h1_in,
    h2_out,
    h2_in,
    g_out,
    g_in,
):
    r = lax.axis_index("row")
    c = lax.axis_index("col")
    other = c // 2
    n_d = depot.shape[0]
    n_z = zone.shape[0]
    n_h1 = send_h1.shape[1]
    n_h2 = side_hub.shape[0] // LANES

    bigs = [
        pltpu.make_async_copy(src, dst, load_sem.at[n])
        for n, (src, dst) in enumerate(
            (
                (theta_one, th1),
                (cost_one, co1),
                (theta_two, th2),
                (cost_two, co2),
                (cot_one, ct1),
                (cot_two, ct2),
            )
        )
    ]
    smalls = [
        pltpu.make_async_copy(src, dst, small_sem.at[n])
        for n, (src, dst) in enumerate(
            (
                (depot_hbm, depot),
                (hub_hbm, hub),
                (zone_hbm, zone),
                (capacity_hbm, capacity),
                (supply_hbm, supply),
                (demand_hbm, demand),
                (cot_depot_hbm, cot_depot),
                (cot_hub_hbm, cot_hub),
                (cot_zone_hbm, cot_zone),
            )
        )
    ]
    for copy in smalls + bigs:
        copy.start()

    barrier = pltpu.get_barrier_semaphore()

    def signal(rr, cc):
        pl.semaphore_signal(barrier, inc=1, device_id=(rr, cc), device_id_type=MESH)

    def loop(count, body):
        def step(k, carry):
            body(k)
            return carry

        lax.fori_loop(0, count, step, 0)

    @pl.when(r != other)
    def _():
        loop(n_col, lambda k: signal(other, lax.rem(c + k, n_col)))
        for q in range(2):
            loop(n_row, lambda k: signal(lax.rem(r + k, n_row), 2 * r + q))

    @pl.when(r == other)
    def _():
        loop(n_col - 1, lambda k: signal(r, lax.rem(c + k + 1, n_col)))
        loop(n_row - 1, lambda k: signal(lax.rem(r + k + 1, n_row), c))
        loop(n_row, lambda k: signal(lax.rem(r + k, n_row), c + 1 - 2 * lax.rem(c, 2)))

    loop(n_col - 1, lambda k: signal(r, lax.rem(c + k + 1, n_col)))
    loop(n_row - 1, lambda k: signal(lax.rem(r + k + 1, n_row), c))

    for copy in smalls:
        copy.wait()

    def hub_one(ref, j):
        return ref[pl.ds(c * n_h1 + j, 1), :]

    def hub_two(ref, i):
        return ref[pl.ds(r * n_h2 + i, 1), :]

    level_one = [hub_one(capacity, j).astype(F32) for j in range(n_h1)]
    for i in range(n_h2):
        side_cap[pl.ds(i * LANES, LANES), :] = spread(0.25 * hub_two(capacity, i).astype(F32))

    def set_sides(depot_rows, hub_rows):
        for i in range(n_d):
            side_depot[pl.ds(i * LANES, LANES), :] = spread(depot_rows[i])
        for i in range(n_h2):
            side_hub[pl.ds(i * LANES, LANES), :] = spread(hub_rows[i])

    def sweep_one(body, lanes, rows_out, cols_out):
        def block(i, cols):
            cols = list(cols)
            for s in range(LANES // CHUNK):
                rows = pl.ds(pl.multiple_of(i * LANES + s * CHUNK, CHUNK), CHUNK)
                side = side_depot[rows, :]
                total = None
                for j in range(n_h1):
                    keep = mask_one[i, j].astype(F32) * level_one[j]
                    value = body(rows, pl.ds(j * LANES, LANES), keep, side, lanes[j])
                    if rows_out:
                        total = value if total is None else total + value
                    if cols_out:
                        cols[j] = cols[j] + fold(value)
                if rows_out:
                    stage_depot[rows, :] = total
            return tuple(cols)

        zero = jnp.zeros((8, LANES), F32)
        cols = lax.fori_loop(0, n_d, block, (zero,) * n_h1 if cols_out else ())
        return [jnp.sum(v, axis=0, keepdims=True) for v in cols]

    def sweep_two(body, lanes, rows_out, cols_out):
        if cols_out:
            stage_zone[...] = jnp.zeros_like(stage_zone)

        def block(n, carry):
            i = n // (LANES // CHUNK)
            rows = pl.ds(pl.multiple_of(n * CHUNK, CHUNK), CHUNK)
            side = side_hub[rows, :]
            cap = side_cap[rows, :]

            def inner(j, total):
                cols = pl.ds(pl.multiple_of(j * LANES, LANES), LANES)
                keep = mask_two[i, j].astype(F32) * cap
                value = body(rows, cols, keep, side, lanes(j))
                if cols_out:
                    stage_zone[j] = stage_zone[j] + fold(value)
                return total + value if rows_out else total

            total = lax.fori_loop(0, n_z, inner, jnp.zeros((CHUNK, LANES), F32) if rows_out else 0)
            if rows_out:
                stage_hub[rows, :] = total
            return carry

        lax.fori_loop(0, n_h2 * (LANES // CHUNK), block, 0)

    def row_totals(stage, count):
        return [
            jnp.sum(jnp.transpose(stage[pl.ds(i * LANES, LANES), :]), axis=0, keepdims=True)
            for i in range(count)
        ]

    def send(t, hubs, cols_one):
        depot_rows = row_totals(stage_depot, n_d)
        for i in range(n_d):
            send_d[t, i : i + 1, :] = depot_rows[i]
        if hubs:
            hub_rows = row_totals(stage_hub, n_h2)
            for i in range(n_h2):
                send_d[t, n_d + i : n_d + i + 1, :] = hub_rows[i]
                send_z[t, n_z + n_h1 + i : n_z + n_h1 + i + 1, :] = hub_rows[i]
                send_h2[t, i // n_h1, i % n_h1 : i % n_h1 + 1, :] = hub_rows[i]
            for j in range(n_h1):
                send_d[t, n_d + n_h2 + j : n_d + n_h2 + j + 1, :] = cols_one[j]
                send_z[t, n_z + j : n_z + j + 1, :] = cols_one[j]
                send_h1[t, j : j + 1, :] = cols_one[j]
        send_z[t, 0:n_z, :] = jnp.sum(stage_zone[...], axis=1)
        if t == 0:
            pl.semaphore_wait(barrier, n_col * 2 + n_row * 3 - 2 - jnp.where(r == other, 2, 0))

        def put(src, dst, out_sem, in_sem, rr, cc):
            pltpu.make_async_remote_copy(
                src_ref=src,
                dst_ref=dst,
                send_sem=out_sem,
                recv_sem=in_sem,
                device_id=(rr, cc),
                device_id_type=MESH,
            ).start()

        if hubs:

            @pl.when(r != other)
            def _():
                loop(
                    n_col,
                    lambda k: put(
                        send_h1.at[t],
                        got_h1.at[t, r, lax.rem(c, 2)],
                        h1_out.at[t],
                        h1_in.at[t],
                        other,
                        lax.rem(c + k, n_col),
                    ),
                )

            for q in range(2):

                @pl.when(2 * r + q != c)
                def _():
                    loop(
                        n_row,
                        lambda k: put(
                            send_h2.at[t, q],
                            got_h2.at[t, c],
                            h2_out.at[t],
                            h2_in.at[t],
                            lax.rem(r + k, n_row),
                            2 * r + q,
                        ),
                    )

        loop(
            n_col - 1,
            lambda k: put(
                send_d.at[t], got_d.at[t, c], d_out.at[t], d_in.at[t], r, lax.rem(c + k + 1, n_col)
            ),
        )
        loop(
            n_row - 1,
            lambda k: put(
                send_z.at[t], got_z.at[t, r], z_out.at[t], z_in.at[t], lax.rem(r + k + 1, n_row), c
            ),
        )
        got_d[t, c] = send_d[t]
        got_z[t, r] = send_z[t]

    def arrived(ref, sem):
        pltpu.make_async_copy(ref, ref, sem).wait()

    def receive(t, hubs):
        arrived(got_d.at[t, pl.ds(0, n_col - 1)], d_in.at[t])
        arrived(got_z.at[t, pl.ds(0, n_row - 1)], z_in.at[t])
        all_d = jnp.sum(got_d[t], axis=0)
        all_z = jnp.sum(got_z[t], axis=0)
        depot_sum = all_d[0:n_d]
        zone_sum = all_z[0:n_z]
        if not hubs:
            return depot_sum, zone_sum, None, None
        arrived(got_h1.at[t, pl.ds(0, n_row - 1)], h1_in.at[t])
        arrived(got_h2.at[t, pl.ds(0, n_col - 1)], h2_in.at[t])
        for q in range(2):
            got_h1[t, r, q] = got_d[t, 2 * r + q, n_d + n_h2 : n_d + n_h2 + n_h1]
        start = n_z + n_h1

        @pl.when(lax.rem(c, 2) == 0)
        def _():
            got_h2[t, c] = got_z[t, other, start : start + n_h1]

        @pl.when(lax.rem(c, 2) == 1)
        def _():
            got_h2[t, c] = got_z[t, other, start + n_h1 : start + 2 * n_h1]

        one_here = all_z[n_z : n_z + n_h1] - jnp.sum(got_h2[t], axis=0)
        ones = jnp.sum(got_h1[t], axis=0)
        two_here = [
            ones[i // n_h1, i % n_h1 : i % n_h1 + 1] - all_d[n_d + i : n_d + i + 1] for i in range(n_h2)
        ]
        one_here = [one_here[j : j + 1] for j in range(n_h1)]
        return depot_sum, zone_sum, one_here, two_here

    def rows_of(value):
        return [value[i : i + 1] for i in range(value.shape[0])]

    hub_a = [hub_one(hub, j) for j in range(n_h1)]
    hub_b = [hub_two(hub, i) for i in range(n_h2)]
    depot_old = depot[...]
    zone_old = zone[...]
    set_sides(rows_of(0.25 * depot_old), [0.25 * v for v in hub_b])
    stage_lane = send_z.at[0]
    stage_lane[0:n_z, :] = 0.25 * zone_old

    def first_one(rows, cols, keep, side, lane):
        old = 0.5 * th1[rows, cols].astype(F32)
        cost = 0.25 * co1[rows, cols].astype(F32)
        new = old - cost - side - lane
        t_new = jnp.tanh(new)
        a1[rows, cols] = new - cost
        b1[rows, cols] = t_new
        return keep * (0.5 + t_new - 0.5 * jnp.tanh(old))

    def first_two(rows, cols, keep, side, lane):
        old = 0.5 * th2[rows, cols].astype(F32)
        cost = 0.25 * co2[rows, cols].astype(F32)
        new = old - cost + side + lane
        t_new = jnp.tanh(new)
        a2[rows, cols] = new - cost
        b2[rows, cols] = t_new
        return keep * (0.5 + t_new - 0.5 * jnp.tanh(old))

    def lane_rows(ref):
        return lambda j: ref[pl.ds(j, 1), :]

    bigs[0].wait()
    bigs[1].wait()
    cols_one = sweep_one(first_one, [0.25 * v for v in hub_a], True, True)
    bigs[2].wait()
    bigs[3].wait()
    sweep_two(first_two, lane_rows(stage_lane), True, True)
    send(0, True, cols_one)
    depot_sum, zone_sum, one_here, two_here = receive(0, True)

    supply_level = 0.5 * supply[...].astype(F32)
    demand_level = 0.125 * demand[...].astype(F32)
    grow_depot_0 = jnp.exp(STEP * (depot_sum * (1.0 / HUB) - supply_level))
    grow_zone_0 = jnp.exp(STEP * (demand_level - zone_sum * (1.0 / HUB)))
    depot_0 = depot_old * grow_depot_0
    zone_0 = zone_old * grow_zone_0
    hub_a = [v + s * (HUB_RATE / DEP) for v, s in zip(hub_a, one_here)]
    hub_b = [v + s * (HUB_RATE / DEP) for v, s in zip(hub_b, two_here)]

    set_sides(rows_of(0.25 * depot_0), [0.25 * v for v in hub_b])
    stage_lane = send_z.at[1]
    stage_lane[0:n_z, :] = 0.25 * zone_0

    def second_one(rows, cols, keep, side, lane):
        t_new = jnp.tanh(a1[rows, cols] - side - lane)
        a1[rows, cols] = t_new
        return keep * (0.5 + t_new - 0.5 * b1[rows, cols])

    def second_two(rows, cols, keep, side, lane):
        t_new = jnp.tanh(a2[rows, cols] + side + lane)
        a2[rows, cols] = t_new
        return keep * (0.5 + t_new - 0.5 * b2[rows, cols])

    sweep_one(second_one, [0.25 * v for v in hub_a], True, False)
    sweep_two(second_two, lane_rows(stage_lane), False, True)
    send(1, False, None)
    bigs[4].wait()
    bigs[5].wait()
    depot_sum, zone_sum, _, _ = receive(1, False)
    grow_depot_1 = jnp.exp(STEP * (depot_sum * (1.0 / HUB) - supply_level))
    grow_zone_1 = jnp.exp(STEP * (demand_level - zone_sum * (1.0 / HUB)))

    adj_depot = cot_depot[...]
    adj_zone = cot_zone[...]
    adj_a = [hub_one(cot_hub, j) for j in range(n_h1)]
    adj_b = [hub_two(cot_hub, i) for i in range(n_h2)]
    push_depot = adj_depot * (depot_0 * grow_depot_1) * (STEP / HUB)
    push_zone = -adj_zone * (zone_0 * grow_zone_1) * (STEP / HUB)
    set_sides(rows_of(push_depot), [-v * (HUB_RATE / DEP) for v in adj_b])
    stage_lane = send_z.at[2]
    stage_lane[0:n_z, :] = push_zone

    def third(ct, a, b, total_out, state_out):
        def body(rows, cols, keep, side, lane):
            weight = side + lane
            quarter = 0.25 * keep
            t_new = a[rows, cols]
            t_old = b[rows, cols]
            total = (quarter * (1.0 - t_new * t_new)) * (ct[rows, cols].astype(F32) + 2.0 * weight)
            slope_old = quarter * (1.0 - t_old * t_old)
            state = total - weight * slope_old
            b[rows, cols] = slope_old
            state_out[rows, cols] = state
            total_out[rows, cols] = -STEP * (total + state)
            return total

        return body

    cols_one = sweep_one(
        third(ct1, a1, b1, grad_cost_one, grad_one), [v * (HUB_RATE / DEP) for v in adj_a], True, True
    )
    sweep_two(third(ct2, a2, b2, grad_cost_two, grad_two), lane_rows(stage_lane), True, True)
    send(2, True, cols_one)

    def start_slope(th, a):
        def body(rows, cols, keep, side, lane):
            t_old = jnp.tanh(0.5 * th[rows, cols].astype(F32))
            a[rows, cols] = (0.25 * keep) * (1.0 - t_old * t_old)

        return body

    sweep_one(start_slope(th1, a1), [None] * n_h1, False, False)
    sweep_two(start_slope(th2, a2), lambda j: None, False, False)
    depot_sum, zone_sum, one_here, two_here = receive(2, True)
    adj_depot = adj_depot * grow_depot_1 - STEP * depot_sum
    adj_zone = adj_zone * grow_zone_1 + STEP * zone_sum
    adj_a = [v - STEP * s for v, s in zip(adj_a, one_here)]
    adj_b = [v - STEP * s for v, s in zip(adj_b, two_here)]

    push_depot = adj_depot * depot_0 * (STEP / HUB)
    push_zone = -adj_zone * zone_0 * (STEP / HUB)
    set_sides(rows_of(push_depot), [-v * (HUB_RATE / DEP) for v in adj_b])
    stage_lane = send_z.at[3]
    stage_lane[0:n_z, :] = push_zone

    def fourth(a, b, total_out, state_out):
        def body(rows, cols, keep, side, lane):
            weight = side + lane
            part = weight * b[rows, cols]
            total = state_out[rows, cols] + 2.0 * part
            state_out[rows, cols] = total - weight * a[rows, cols]
            total_out[rows, cols] = total_out[rows, cols] - part
            return total

        return body

    cols_one = sweep_one(
        fourth(a1, b1, grad_cost_one, grad_one), [v * (HUB_RATE / DEP) for v in adj_a], True, True
    )
    sweep_two(fourth(a2, b2, grad_cost_two, grad_two), lane_rows(stage_lane), True, True)
    send(3, True, cols_one)
    depot_sum, zone_sum, one_here, two_here = receive(3, True)
    grad_depot[...] = adj_depot * grow_depot_0 - STEP * depot_sum
    grad_zone[...] = adj_zone * grow_zone_0 + STEP * zone_sum
    for i in range(n_h2):
        got_g[r, i : i + 1, :] = adj_b[i] - STEP * two_here[i]

    def give(k):
        pltpu.make_async_remote_copy(
            src_ref=got_g.at[r],
            dst_ref=got_g.at[r],
            send_sem=g_out.at[0],
            recv_sem=g_in.at[0],
            device_id=(lax.rem(r + k + 1, n_row), c),
            device_id_type=MESH,
        ).start()

    loop(n_row - 1, give)
    arrived(got_g.at[pl.ds(0, n_row - 1)], g_in.at[0])
    for k in range(n_row):
        grad_hub[k * n_h2 : (k + 1) * n_h2, :] = got_g[k]

    arrived(got_g.at[pl.ds(0, n_row - 1)], g_out.at[0])
    for t in range(4):
        arrived(got_d.at[t, pl.ds(0, n_col - 1)], d_out.at[t])
        arrived(got_z.at[t, pl.ds(0, n_row - 1)], z_out.at[t])
        if t != 1:

            @pl.when(r != other)
            def _():
                arrived(got_h2.at[t], h1_out.at[t])
                arrived(got_h2.at[t], h2_out.at[t])

            @pl.when(r == other)
            def _():
                arrived(got_h2.at[t, pl.ds(0, n_row)], h2_out.at[t])


def on_device(n_row, n_col, *args):
    (theta_one, theta_two, cost_one, cost_two, depot, hub, zone, mask_one, mask_two) = args[:9]
    (supply, demand, capacity, cot_one, cot_two, cot_depot, cot_hub, cot_zone) = args[9:]

    def packed(vector):
        return vector.reshape(vector.shape[0] // LANES, LANES)

    depots, hubs_one = theta_one.shape
    hubs_two, zones = theta_two.shape
    n_d, n_z, n_h = depots // LANES, zones // LANES, hub.shape[0] // LANES
    n_h1, n_h2 = hubs_one // LANES, hubs_two // LANES
    rows_d = -(-(n_d + n_h1 + n_h2) // 8) * 8
    rows_z = -(-(n_z + n_h1 + n_h2) // 8) * 8
    big_one, big_two = (depots, hubs_one), (hubs_two, zones)
    any_spec = pl.BlockSpec(memory_space=pl.ANY)
    smem = pl.BlockSpec(memory_space=pltpu.SMEM)
    vmem = pl.BlockSpec(memory_space=pltpu.VMEM)
    dma = pltpu.SemaphoreType.DMA
    in_specs = [any_spec] * 7 + [smem] * 2 + [any_spec] * 8
    outs = pl.pallas_call(
        functools.partial(kernel, n_row, n_col),
        out_shape=[
            jax.ShapeDtypeStruct(big_one, F32),
            jax.ShapeDtypeStruct(big_two, F32),
            jax.ShapeDtypeStruct(big_one, F32),
            jax.ShapeDtypeStruct(big_two, F32),
            jax.ShapeDtypeStruct((n_d, LANES), F32),
            jax.ShapeDtypeStruct((n_h, LANES), F32),
            jax.ShapeDtypeStruct((n_z, LANES), F32),
        ],
        in_specs=in_specs,
        out_specs=[vmem] * 7,
        scratch_shapes=[
            pltpu.VMEM(big_one, jnp.bfloat16),
            pltpu.VMEM(big_two, jnp.bfloat16),
            pltpu.VMEM(big_one, jnp.bfloat16),
            pltpu.VMEM(big_two, jnp.bfloat16),
            pltpu.VMEM(big_one, jnp.bfloat16),
            pltpu.VMEM(big_two, jnp.bfloat16),
            pltpu.VMEM((n_d, LANES), F32),
            pltpu.VMEM((n_h, LANES), F32),
            pltpu.VMEM((n_z, LANES), F32),
            pltpu.VMEM((n_d, LANES), jnp.int32),
            pltpu.VMEM((n_z, LANES), jnp.int32),
            pltpu.VMEM((n_h, LANES), jnp.int32),
            pltpu.VMEM((n_d, LANES), F32),
            pltpu.VMEM((n_h, LANES), F32),
            pltpu.VMEM((n_z, LANES), F32),
            pltpu.VMEM(big_one, F32),
            pltpu.VMEM(big_two, F32),
            pltpu.VMEM(big_one, F32),
            pltpu.VMEM(big_two, F32),
            pltpu.VMEM((depots, LANES), F32),
            pltpu.VMEM((hubs_two, LANES), F32),
            pltpu.VMEM((hubs_two, LANES), F32),
            pltpu.VMEM((depots, LANES), F32),
            pltpu.VMEM((hubs_two, LANES), F32),
            pltpu.VMEM((n_z, 8, LANES), F32),
            pltpu.VMEM((4, rows_d, LANES), F32),
            pltpu.VMEM((4, rows_z, LANES), F32),
            pltpu.VMEM((4, n_h1, LANES), F32),
            pltpu.VMEM((4, 2, n_h1, LANES), F32),
            pltpu.VMEM((4, n_col, rows_d, LANES), F32),
            pltpu.VMEM((4, n_row, rows_z, LANES), F32),
            pltpu.VMEM((4, n_row, 2, n_h1, LANES), F32),
            pltpu.VMEM((4, n_col, n_h1, LANES), F32),
            pltpu.VMEM((n_row, n_h2, LANES), F32),
            dma((6,)),
            dma((9,)),
            dma((4,)),
            dma((4,)),
            dma((4,)),
            dma((4,)),
            dma((4,)),
            dma((4,)),
            dma((4,)),
            dma((4,)),
            dma((1,)),
            dma((1,)),
        ],
        compiler_params=pltpu.CompilerParams(
            collective_id=0, has_side_effects=True, vmem_limit_bytes=60 * 1024 * 1024
        ),
    )(
        theta_one,
        theta_two,
        cost_one,
        cost_two,
        packed(depot),
        packed(hub),
        packed(zone),
        mask_one,
        mask_two,
        packed(supply),
        packed(demand),
        packed(capacity),
        cot_one,
        cot_two,
        packed(cot_depot),
        packed(cot_hub),
        packed(cot_zone),
    )
    return tuple(outs[:4]) + tuple(v.reshape(-1) for v in outs[4:])


def solution(mesh):
    n_row, n_col = mesh.shape["row"], mesh.shape["col"]
    block, by_row, by_col = P("row", "col"), P("row"), P("col")
    return jax.shard_map(
        functools.partial(on_device, n_row, n_col),
        mesh=mesh,
        in_specs=(
            (block,) * 4 + (by_row, P(), by_col, block, block, by_row, by_col, P(), block, block)
            + (by_row, P(), by_col)
        ),
        out_specs=(block,) * 4 + (by_row, P(), by_col),
        check_vma=False,
    )
```

```python
import functools
import types

import jax
import jax.numpy as jnp
from jax import lax
from jax.experimental import pallas as pl
from jax.experimental.pallas import tpu as pltpu
from jax.sharding import PartitionSpec as P

DEP = 8192
HUB = 4096
LANES = 128
STEP = 0.5
HUB_RATE = 4.0
CHUNK = 32
WIDE = 16
MESH = pl.DeviceIdType.MESH
F32 = jnp.float32
FIRST, SECOND, LINEAR, THIRD, FINAL_HUB, FOURTH = range(6)


def fold(values):
    return jnp.sum(values.reshape(values.shape[0] // 8, 8, LANES), axis=0)


def spread(row):
    return jnp.transpose(jnp.broadcast_to(row, (LANES, LANES)))


def loop(count, body):
    def step(k, carry):
        body(k)
        return carry

    lax.fori_loop(0, count, step, 0)


def arrived(ref, sem):
    pltpu.make_async_copy(ref, ref, sem).wait()


def main_kernel(n_row, n_col, n_in, n_out, tree, *refs):
    (theta_one, theta_two, cost_one, cost_two, depot_hbm, hub_hbm, zone_hbm, mask_one_hbm, mask_two_hbm) = refs[:9]
    (supply_hbm, demand_hbm, capacity_hbm, cot_one, cot_two) = refs[9:14]
    (cot_depot_hbm, cot_hub_hbm, cot_zone_hbm) = refs[14:17]
    (grad_one, grad_two, grad_cost_one, grad_cost_two, grad_depot, grad_hub, grad_zone) = refs[n_in : n_in + n_out]
    m = types.SimpleNamespace(**jax.tree.unflatten(tree, refs[n_in + n_out :]))

    r = lax.axis_index("row")
    c = lax.axis_index("col")
    other = c // 2
    n_d = m.depot.shape[0]
    n_z = m.zone.shape[0]
    n_h1 = theta_one.shape[1] // LANES
    n_h2 = theta_two.shape[0] // LANES
    halves = LANES // CHUNK

    def load(src, dst, sem):
        copy = pltpu.make_async_copy(src, dst, sem)
        copy.start()
        return copy

    mask_one, mask_two = m.mask_one, m.mask_two
    pairs = (
        (depot_hbm, m.depot),
        (capacity_hbm, m.capacity),
        (hub_hbm, m.hub),
        (zone_hbm, m.zone),
        (mask_one_hbm, mask_one),
        (mask_two_hbm, mask_two),
    )
    smalls = [load(src, dst, m.small_sem.at[n]) for n, (src, dst) in enumerate(pairs)]
    loads_one = [load(theta_one, m.th1, m.load_sem.at[0]), load(cost_one, m.co1, m.load_sem.at[1])]

    def load_two(i):
        rows = pl.ds(i * LANES, LANES)
        pairs = ((theta_two, m.th2), (cost_two, m.co2))
        return [load(src.at[rows], dst.at[rows], m.two_sem.at[i, n]) for n, (src, dst) in enumerate(pairs)]

    early = n_h2 // 2
    loads_two = [load_two(i) for i in range(early)]

    barrier = pltpu.get_barrier_semaphore()

    def signal(rr, cc):
        pl.semaphore_signal(barrier, inc=1, device_id=(rr, cc), device_id_type=MESH)

    @pl.when(r != other)
    def _():
        loop(n_col, lambda k: signal(other, lax.rem(c + k, n_col)))
        for q in range(2):
            loop(n_row, lambda k: signal(lax.rem(r + k, n_row), 2 * r + q))

    @pl.when(r == other)
    def _():
        loop(n_col - 1, lambda k: signal(r, lax.rem(c + k + 1, n_col)))
        loop(n_row - 1, lambda k: signal(lax.rem(r + k + 1, n_row), c))
        loop(n_row, lambda k: signal(lax.rem(r + k, n_row), c + 1 - 2 * lax.rem(c, 2)))

    loop(n_col - 1, lambda k: signal(r, lax.rem(c + k + 1, n_col)))
    loop(n_row - 1, lambda k: signal(lax.rem(r + k + 1, n_row), c))

    for copy in smalls:
        copy.wait()

    def hub_one(ref):
        return jnp.concatenate([ref[pl.ds(c * n_h1 + j, 1), :] for j in range(n_h1)], axis=0)

    def hub_two(ref):
        return jnp.concatenate([ref[pl.ds(r * n_h2 + i, 1), :] for i in range(n_h2)], axis=0)

    def set_side(ref, packed):
        for i in range(packed.shape[0]):
            ref[i * LANES : (i + 1) * LANES, :] = spread(packed[i : i + 1])

    level_one = hub_one(m.capacity).astype(F32)
    set_side(m.side_cap, 0.25 * hub_two(m.capacity).astype(F32))

    def sweep_one(body, n_rows, n_cols):
        def block(i, cols):
            cols = list(cols)
            writes = []
            totals = []
            for s in range(halves):
                rows = pl.ds(pl.multiple_of(i * LANES + s * CHUNK, CHUNK), CHUNK)
                total = [None] * n_rows
                for j in range(n_h1):
                    keep = mask_one[j, i].astype(F32) * level_one[j : j + 1]
                    lanes = pl.ds(j * LANES, LANES)
                    by_row, by_col, stores = body(rows, lanes, keep, j)
                    for n, value in enumerate(by_row):
                        total[n] = value if total[n] is None else total[n] + value
                    for n, value in enumerate(by_col):
                        cols[n * n_h1 + j] = cols[n * n_h1 + j] + fold(value)
                    writes += [(ref, rows, lanes, value) for ref, value in stores]
                totals.append((rows, total))
            for ref, rows, lanes, value in writes:
                ref[rows, lanes] = value
            for rows, total in totals:
                for n in range(n_rows):
                    m.stage_depot[n, rows, :] = total[n]
            return tuple(cols)

        zero = jnp.zeros((8, LANES), F32)
        cols = lax.fori_loop(0, n_d, block, (zero,) * (n_h1 * n_cols))
        cols = [jnp.sum(v, axis=0, keepdims=True) for v in cols]
        return [jnp.concatenate(cols[n * n_h1 : (n + 1) * n_h1], axis=0) for n in range(n_cols)]

    def sweep_two(body, n_rows, n_cols, before=None):
        for n in range(n_cols):
            m.stage_zone[n] = jnp.zeros(m.stage_zone.shape[1:], F32)

        def block(n, i):
            rows = pl.ds(pl.multiple_of(n * CHUNK, CHUNK), CHUNK)
            cap = m.side_cap[rows, :]

            def inner(jj, totals):
                totals = list(totals)
                writes = []
                for q in range(WIDE):
                    j = jj * WIDE + q
                    lanes = pl.ds(pl.multiple_of(j * LANES, LANES), LANES)
                    keep = mask_two[i, j].astype(F32) * cap
                    by_row, by_col, stores = body(rows, lanes, keep, j)
                    for k, value in enumerate(by_row):
                        totals[k] = totals[k] + value
                    writes += [(m.stage_zone, (k, j), fold(value)) for k, value in enumerate(by_col)]
                    writes += [(ref, (rows, lanes), value) for ref, value in stores]
                for ref, where, value in writes:
                    if ref is m.stage_zone:
                        value = ref[where] + value
                    ref[where] = value
                return tuple(totals)

            zero = jnp.zeros((CHUNK, LANES), F32)
            totals = lax.fori_loop(0, n_z // WIDE, inner, (zero,) * n_rows)
            for k in range(n_rows):
                m.stage_hub[k, rows, :] = totals[k]

        if before is None:
            loop(n_h2 * halves, lambda n: block(n, n // halves))
        else:
            for i in range(n_h2):
                before(i)
                loop(halves, lambda s: block(i * halves + s, i))

    def packed_rows(stage, n, count):
        parts = [
            jnp.sum(jnp.transpose(stage[n, i * LANES : (i + 1) * LANES, :]), axis=0, keepdims=True)
            for i in range(count)
        ]
        return jnp.concatenate(parts, axis=0)

    def depot_rows(n):
        return packed_rows(m.stage_depot, n, n_d)

    def hub_rows(n):
        return packed_rows(m.stage_hub, n, n_h2)

    def zone_cols(n):
        return jnp.sum(m.stage_zone[n], axis=1)

    def fill(ref, *parts):
        start = 0
        for part in parts:
            ref[start : start + part.shape[0], :] = part
            start += part.shape[0]

    def put(src, dst, out_sem, in_sem, rr, cc):
        pltpu.make_async_remote_copy(
            src_ref=src,
            dst_ref=dst,
            send_sem=out_sem,
            recv_sem=in_sem,
            device_id=(rr, cc),
            device_id_type=MESH,
        ).start()

    def share_cols(t):
        src, got = m.send_d[t], m.got_d[t]
        sems = m.d_out.at[t], m.d_in.at[t]
        loop(n_col - 1, lambda k: put(src, got.at[c], *sems, r, lax.rem(c + k + 1, n_col)))
        got[c] = src[...]

    def share_rows(t):
        src, got = m.send_z[t], m.got_z[t]
        sems = m.z_out.at[t], m.z_in.at[t]
        loop(n_row - 1, lambda k: put(src, got.at[r], *sems, lax.rem(r + k + 1, n_row), c))
        got[r] = src[...]

    def share_one(t):
        sems = m.h1_out.at[t], m.h1_in.at[t]

        @pl.when(r != other)
        def _():
            loop(
                n_col,
                lambda k: put(
                    m.send_h1[t],
                    m.got_h1[t].at[r, lax.rem(c, 2)],
                    *sems,
                    other,
                    lax.rem(c + k, n_col),
                ),
            )

    def share_two(t):
        sems = m.h2_out.at[t], m.h2_in.at[t]
        for q in range(2):

            @pl.when(2 * r + q != c)
            def _():
                loop(
                    n_row,
                    lambda k: put(
                        m.send_h2[t].at[q], m.got_h2[t].at[c], *sems, lax.rem(r + k, n_row), 2 * r + q
                    ),
                )

    def from_cols(t):
        got = m.got_d[t]
        arrived(got.at[pl.ds(0, n_col - 1)], m.d_in.at[t])
        return jnp.sum(got[...], axis=0)

    def from_rows(t):
        got = m.got_z[t]
        arrived(got.at[pl.ds(0, n_row - 1)], m.z_in.at[t])
        return jnp.sum(got[...], axis=0)

    def send_hubs(t, one, two, lead_d, lead_z):
        fill(m.send_h1[t], one)
        for q in range(2):
            m.send_h2[t][q] = two[q * n_h1 : (q + 1) * n_h1]
        fill(m.send_d[t], *lead_d, two, one)
        fill(m.send_z[t], *lead_z, one, two)

    def receive_one(t, start):
        got = m.got_h1[t]
        size = got.shape[2]
        arrived(got.at[pl.ds(0, n_row - 1)], m.h1_in.at[t])
        for q in range(2):
            got[r, q] = m.got_d[t][2 * r + q, start : start + size]
        return jnp.sum(got[...], axis=0)

    def receive_two(t, start):
        got = m.got_h2[t]
        arrived(got.at[pl.ds(0, n_col - 1)], m.h2_in.at[t])
        for q in range(2):

            @pl.when(lax.rem(c, 2) == q)
            def _():
                got[c] = m.got_z[t][other, start + q * n_h1 : start + (q + 1) * n_h1]

        return jnp.sum(got[...], axis=0)

    def receive_hubs(t, all_d, all_z, lead_d, lead_z):
        ones = receive_one(t, lead_d + n_h2)
        one_here = all_z[lead_z : lead_z + n_h1] - receive_two(t, lead_z + n_h1)
        ones = jnp.concatenate([ones[0], ones[1]], axis=0)
        return one_here, ones - all_d[lead_d : lead_d + n_h2]

    hub_a = hub_one(m.hub)
    hub_b = hub_two(m.hub)
    depot_old = m.depot[...]
    zone_old = m.zone[...]
    set_side(m.side_depot, 0.25 * depot_old)
    set_side(m.side_hub, 0.25 * hub_b)
    m.lane_zone[0] = 0.25 * zone_old
    lane_one = 0.25 * hub_a

    def first(th, co, a, b, z, sign, weights):
        def body(rows, lanes, keep, j):
            old = 0.5 * th[rows, lanes].astype(F32)
            cost = 0.25 * co[rows, lanes].astype(F32)
            new = old - cost + sign * weights(rows, j)
            t_old = jnp.tanh(old)
            t_new = jnp.tanh(new)
            value = keep * (0.5 + t_new - 0.5 * t_old)
            return [value], [value], [(a, new - cost), (b, t_new), (z, t_old)]

        return body

    for copy in loads_one:
        copy.wait()
    loads_two += [load_two(i) for i in range(early, n_h2)]
    (one,) = sweep_one(
        first(
            m.th1,
            m.co1,
            m.a1,
            m.b1,
            m.z1,
            -1.0,
            lambda rows, j: m.side_depot[rows, :] + lane_one[j : j + 1],
        ),
        1,
        1,
    )

    def zone_lane(k, j):
        return m.lane_zone[k, pl.ds(j, 1), :]

    def wait_two(i):
        for copy in loads_two[i]:
            copy.wait()

    sweep_two(
        first(
            m.th2,
            m.co2,
            m.a2,
            m.b2,
            m.z2,
            1.0,
            lambda rows, j: m.side_hub[rows, :] + zone_lane(0, j),
        ),
        1,
        1,
        wait_two,
    )
    pairs = (
        (cot_depot_hbm, m.cot_depot),
        (cot_hub_hbm, m.cot_hub),
        (cot_zone_hbm, m.cot_zone),
        (supply_hbm, m.supply),
        (demand_hbm, m.demand),
    )
    smalls = [load(src, dst, m.small_sem.at[n + 6]) for n, (src, dst) in enumerate(pairs)]
    late = [load(cot_one, m.ct1, m.load_sem.at[2]), load(cot_two, m.ct2, m.load_sem.at[3])]
    send_hubs(FIRST, one, hub_rows(0), [depot_rows(0)], [zone_cols(0)])
    pl.semaphore_wait(barrier, n_col * 2 + n_row * 3 - 2 - jnp.where(r == other, 2, 0))
    share_one(FIRST)
    share_two(FIRST)
    share_cols(FIRST)
    share_rows(FIRST)

    for copy in smalls:
        copy.wait()
    adj_depot = m.cot_depot[...]
    adj_zone = m.cot_zone[...]
    adj_a = hub_one(m.cot_hub)
    adj_b = hub_two(m.cot_hub)
    push_a = adj_a * (HUB_RATE / DEP)
    push_b = adj_b * (-HUB_RATE / DEP)
    set_side(m.side_push, push_b)
    supply_level = 0.5 * m.supply[...].astype(F32)
    demand_level = 0.125 * m.demand[...].astype(F32)

    def slopes(b, z, keep, rows, lanes):
        t_new = b[rows, lanes]
        t_old = z[rows, lanes]
        quarter = 0.25 * keep
        square = t_new * t_new
        rest = 1.0 - square
        slope = quarter * rest
        return keep * (0.5 - 0.5 * t_new), slope, quarter * (rest - square + t_old * t_old)

    def window_one(rows, lanes, keep, j):
        past, slope, mixed = slopes(m.b1, m.z1, keep, rows, lanes)
        return [past, slope, slope * push_a[j : j + 1]], [slope], [(m.b1, slope), (m.z1, mixed)]

    def window_two(rows, lanes, keep, j):
        past, slope, mixed = slopes(m.b2, m.z2, keep, rows, lanes)
        return [slope], [past, slope, slope * m.side_push[rows, :]], [(m.b2, slope), (m.z2, mixed)]

    (slope_a,) = sweep_one(window_one, 3, 1)
    past_depot, slope_depot, pushed_depot = depot_rows(0), depot_rows(1), depot_rows(2)
    sweep_two(window_two, 1, 3)
    past_zone, slope_zone, pushed_zone = zone_cols(0), zone_cols(1), zone_cols(2)
    slope_b = hub_rows(0)

    all_d = from_cols(FIRST)
    all_z = from_rows(FIRST)
    one_here, two_here = receive_hubs(FIRST, all_d, all_z, n_d, n_z)
    grow_depot_0 = jnp.exp(STEP * (all_d[0:n_d] * (1.0 / HUB) - supply_level))
    grow_zone_0 = jnp.exp(STEP * (demand_level - all_z[0:n_z] * (1.0 / HUB)))
    depot_0 = depot_old * grow_depot_0
    zone_0 = zone_old * grow_zone_0
    hub_a = hub_a + one_here * (HUB_RATE / DEP)
    hub_b = hub_b + two_here * (HUB_RATE / DEP)

    set_side(m.side_depot, 0.25 * depot_0)
    set_side(m.side_hub, 0.25 * hub_b)
    m.lane_zone[0] = 0.25 * zone_0
    lane_one_next = 0.25 * hub_a

    def second_one(rows, lanes, keep, j):
        t_new = jnp.tanh(m.a1[rows, lanes] - (m.side_depot[rows, :] + lane_one_next[j : j + 1]))
        return [keep * t_new], [], [(m.a1, t_new)]

    def second_two(rows, lanes, keep, j):
        t_new = jnp.tanh(m.a2[rows, lanes] + (m.side_hub[rows, :] + zone_lane(0, j)))
        return [], [keep * t_new], [(m.a2, t_new)]

    sweep_one(second_one, 1, 0)
    sweep_two(second_two, 0, 1)
    fill(m.send_d[1], depot_rows(0) + past_depot)
    fill(m.send_z[1], zone_cols(0) + past_zone)
    share_cols(SECOND)
    share_rows(SECOND)

    for copy in late:
        copy.wait()

    def linear_one(rows, lanes, keep, j):
        t_new = m.a1[rows, lanes]
        beta = (0.25 * keep) * (1.0 - t_new * t_new)
        alpha = beta * (m.ct1[rows, lanes].astype(F32) + 2.0 * push_a[j : j + 1])
        return [alpha, beta], [alpha], [(m.a1, beta), (m.w1, alpha)]

    def linear_two(rows, lanes, keep, j):
        t_new = m.a2[rows, lanes]
        beta = (0.25 * keep) * (1.0 - t_new * t_new)
        alpha = beta * (m.ct2[rows, lanes].astype(F32) + 2.0 * m.side_push[rows, :])
        return [alpha], [alpha, beta], [(m.a2, beta), (m.w2, alpha)]

    (alpha_a,) = sweep_one(linear_one, 2, 1)
    alpha_depot, beta_depot = depot_rows(0), depot_rows(1)
    sweep_two(linear_two, 1, 2)
    alpha_zone, beta_zone = zone_cols(0), zone_cols(1)
    alpha_b = hub_rows(0)
    fill(m.send_d[2], alpha_depot, beta_depot)
    fill(m.send_z[2], alpha_zone, beta_zone)
    share_cols(LINEAR)
    share_rows(LINEAR)

    grow_depot_1 = jnp.exp(STEP * (from_cols(SECOND) * (1.0 / HUB) - supply_level))
    grow_zone_1 = jnp.exp(STEP * (demand_level - from_rows(SECOND) * (1.0 / HUB)))

    push_depot = adj_depot * (depot_0 * grow_depot_1) * (STEP / HUB)
    push_zone = -adj_zone * (zone_0 * grow_zone_1) * (STEP / HUB)
    set_side(m.side_depot, 2.0 * push_depot)
    m.lane_zone[0] = 2.0 * push_zone

    def third_one(rows, lanes, keep, j):
        return [], [m.a1[rows, lanes] * m.side_depot[rows, :]], []

    def third_two(rows, lanes, keep, j):
        return [m.a2[rows, lanes] * zone_lane(0, j)], [], []

    (one,) = sweep_one(third_one, 0, 1)
    sweep_two(third_two, 1, 0)
    one = one + alpha_a
    two = hub_rows(0) + alpha_b
    send_hubs(THIRD, one, two, [], [])
    share_one(THIRD)
    share_two(THIRD)
    share_cols(THIRD)
    share_rows(THIRD)

    all_d = from_cols(LINEAR)
    all_z = from_rows(LINEAR)
    adj_depot = adj_depot * grow_depot_1 - STEP * (all_d[0:n_d] + 2.0 * push_depot * all_d[n_d : 2 * n_d])
    adj_zone = adj_zone * grow_zone_1 + STEP * (all_z[0:n_z] + 2.0 * push_zone * all_z[n_z : 2 * n_z])
    last_depot = adj_depot * depot_0 * (STEP / HUB)
    last_zone = -adj_zone * zone_0 * (STEP / HUB)
    set_side(m.side_last, last_depot)
    m.lane_zone[1] = last_zone

    def both_one(rows, lanes, keep, j):
        weight = 2.0 * m.side_last[rows, :] - 0.5 * m.side_depot[rows, :]
        return [], [m.b1[rows, lanes] * weight], []

    def both_two(rows, lanes, keep, j):
        return [m.b2[rows, lanes] * (2.0 * zone_lane(1, j) - 0.5 * zone_lane(0, j))], [], []

    (more,) = sweep_one(both_one, 0, 1)
    one = one + more - push_a * slope_a
    sweep_two(both_two, 1, 0)
    two = two + hub_rows(0) - push_b * slope_b
    fill(m.send_h1[4], one, slope_a)
    fill(m.send_d[4], two, slope_b, one, slope_a)
    share_one(FINAL_HUB)
    share_cols(FINAL_HUB)

    def state(total, weight, last, slope, mixed):
        part = weight * slope
        return total - part + last * mixed, 0.5 * part - total - last * slope

    def state_one(rows, lanes, keep, j):
        twice = m.side_depot[rows, :]
        total = m.w1[rows, lanes] + twice * m.a1[rows, lanes]
        weight = 0.5 * twice + push_a[j : j + 1]
        theta, cost = state(
            total, weight, m.side_last[rows, :], m.b1[rows, lanes], m.z1[rows, lanes]
        )
        return [], [], [(grad_one, theta), (grad_cost_one, cost)]

    def state_two(rows, lanes, keep, j):
        twice = zone_lane(0, j)
        total = m.w2[rows, lanes] + twice * m.a2[rows, lanes]
        weight = 0.5 * twice + m.side_push[rows, :]
        theta, cost = state(total, weight, zone_lane(1, j), m.b2[rows, lanes], m.z2[rows, lanes])
        return [], [], [(grad_two, theta), (grad_cost_two, cost)]

    sweep_one(state_one, 0, 0)
    sweep_two(state_two, 0, 0)

    all_d = from_cols(THIRD)
    all_z = from_rows(THIRD)
    one_here, two_here = receive_hubs(THIRD, all_d, all_z, 0, 0)
    adj_a = adj_a - STEP * one_here
    adj_b = adj_b - STEP * two_here
    last_a = adj_a * (HUB_RATE / DEP)
    last_b = adj_b * (-HUB_RATE / DEP)

    set_side(m.side_hub, last_b)

    def fourth_one(rows, lanes, keep, j):
        return [m.b1[rows, lanes] * last_a[j : j + 1]], [], []

    def fourth_two(rows, lanes, keep, j):
        return [], [m.b2[rows, lanes] * m.side_hub[rows, :]], []

    sweep_one(fourth_one, 1, 0)
    sweep_two(fourth_two, 0, 1)

    def last_sum(alpha, beta, push, slope, pushed, last, value):
        return alpha + 2.0 * push * beta + (2.0 * last - push) * slope - pushed + 2.0 * value

    fill(
        m.send_d[5],
        last_sum(alpha_depot, beta_depot, push_depot, slope_depot, pushed_depot, last_depot, depot_rows(0)),
    )
    fill(
        m.send_z[5],
        last_sum(alpha_zone, beta_zone, push_zone, slope_zone, pushed_zone, last_zone, zone_cols(0)),
    )
    share_cols(FOURTH)
    share_rows(FOURTH)

    all_d = from_cols(FINAL_HUB)
    ones = receive_one(FINAL_HUB, 2 * n_h2)
    sums = jnp.concatenate([ones[0, 0:n_h1], ones[1, 0:n_h1]], axis=0)
    sums_slope = jnp.concatenate([ones[0, n_h1 : 2 * n_h1], ones[1, n_h1 : 2 * n_h1]], axis=0)
    sums = sums - 2.0 * last_b * sums_slope
    two_sum = all_d[0:n_h2] + 2.0 * last_b * all_d[n_h2 : 2 * n_h2]
    got_g = m.got_g
    got_g[r] = adj_b + STEP * (two_sum - sums)
    sems = m.g_out.at[0], m.g_in.at[0]
    loop(n_row - 1, lambda k: put(got_g.at[r], got_g.at[r], *sems, lax.rem(r + k + 1, n_row), c))

    def end_one(rows, lanes, keep, j):
        lane = last_a[j : j + 1]
        theta = grad_one[rows, lanes] + lane * m.z1[rows, lanes]
        cost = grad_cost_one[rows, lanes] - lane * m.b1[rows, lanes]
        return [], [], [(grad_one, theta), (grad_cost_one, cost)]

    def end_two(rows, lanes, keep, j):
        side = m.side_hub[rows, :]
        theta = grad_two[rows, lanes] + side * m.z2[rows, lanes]
        cost = grad_cost_two[rows, lanes] - side * m.b2[rows, lanes]
        return [], [], [(grad_two, theta), (grad_cost_two, cost)]

    sweep_one(end_one, 0, 0)
    sweep_two(end_two, 0, 0)

    grad_depot[...] = adj_depot * grow_depot_0 - STEP * from_cols(FOURTH)
    grad_zone[...] = adj_zone * grow_zone_0 + STEP * from_rows(FOURTH)
    arrived(got_g.at[pl.ds(0, n_row - 1)], m.g_in.at[0])
    for k in range(n_row):
        grad_hub[k * n_h2 : (k + 1) * n_h2, :] = got_g[k]

    arrived(got_g.at[pl.ds(0, n_row - 1)], m.g_out.at[0])
    for t in range(6):
        arrived(m.got_d[t].at[pl.ds(0, n_col - 1)], m.d_out.at[t])
        if t != FINAL_HUB:
            arrived(m.got_z[t].at[pl.ds(0, n_row - 1)], m.z_out.at[t])
        if t in (FIRST, THIRD, FINAL_HUB):

            @pl.when(r != other)
            def _():
                arrived(m.got_h1[t], m.h1_out.at[t])

        if t in (FIRST, THIRD):
            arrived(m.got_h2[t].at[pl.ds(0, n_row)], m.h2_out.at[t])

            @pl.when(r != other)
            def _():
                arrived(m.got_h2[t].at[pl.ds(0, n_row)], m.h2_out.at[t])


def write_kernel(*refs):
    count = (len(refs) - 1) // 2
    sem = refs[-1]
    copies = []
    for src, dst in zip(refs[:count], refs[count:-1]):
        rows = src.shape[0]
        parts = 4 if rows >= 512 else 1
        for n in range(parts):
            piece = pl.ds(n * (rows // parts), rows // parts)
            copies.append(pltpu.make_async_copy(src.at[piece], dst.at[piece], sem.at[len(copies)]))
    for copy in copies:
        copy.start()
    for copy in copies:
        copy.wait()


def on_device(n_row, n_col, *args):
    (theta_one, theta_two, cost_one, cost_two, depot, hub, zone, mask_one, mask_two) = args[:9]
    (supply, demand, capacity, cot_one, cot_two, cot_depot, cot_hub, cot_zone) = args[9:]

    def packed(vector):
        return vector.reshape(vector.shape[0] // LANES, LANES)

    depots, hubs_one = theta_one.shape
    hubs_two, zones = theta_two.shape
    n_d, n_z, n_h = depots // LANES, zones // LANES, hub.shape[0] // LANES
    n_h1, n_h2 = hubs_one // LANES, hubs_two // LANES
    one, two = (depots, hubs_one), (hubs_two, zones)

    def rounded(rows):
        return -(-rows // 8) * 8

    def vec(rows, dtype=F32):
        return pltpu.VMEM((rows, LANES), dtype)

    dma = pltpu.SemaphoreType.DMA
    bf16 = jnp.bfloat16
    hubs = n_h1 + n_h2
    rows_d = [rounded(v) for v in (n_d + hubs, n_d, 2 * n_d, hubs, 2 * hubs, n_d)]
    rows_z = [rounded(v) for v in (n_z + hubs, n_z, 2 * n_z, hubs, 8, n_z)]
    rows_h = [n_h1, 0, 0, n_h1, 2 * n_h1, 0]

    def state():
        return pltpu.VMEM(one, F32)

    def state_two():
        return pltpu.VMEM(two, F32)

    def each(shape_of, rows):
        return [pltpu.VMEM(shape_of(v), F32) if v else None for v in rows]

    scratch = dict(
        th1=pltpu.VMEM(one, bf16),
        th2=pltpu.VMEM(two, bf16),
        co1=pltpu.VMEM(one, bf16),
        co2=pltpu.VMEM(two, bf16),
        ct1=pltpu.VMEM(one, bf16),
        ct2=pltpu.VMEM(two, bf16),
        mask_one=pltpu.SMEM((n_h1, n_d), jnp.int32),
        mask_two=pltpu.SMEM((n_h2, n_z), jnp.int32),
        depot=vec(n_d),
        hub=vec(n_h),
        zone=vec(n_z),
        supply=vec(n_d, jnp.int32),
        demand=vec(n_z, jnp.int32),
        capacity=vec(n_h, jnp.int32),
        cot_depot=vec(n_d),
        cot_hub=vec(n_h),
        cot_zone=vec(n_z),
        side_depot=vec(depots),
        side_last=vec(depots),
        side_hub=vec(hubs_two),
        side_push=vec(hubs_two),
        side_cap=vec(hubs_two),
        lane_zone=pltpu.VMEM((2, n_z, LANES), F32),
        stage_depot=pltpu.VMEM((3, depots, LANES), F32),
        stage_hub=pltpu.VMEM((1, hubs_two, LANES), F32),
        stage_zone=pltpu.VMEM((3, n_z, 8, LANES), F32),
        got_g=pltpu.VMEM((n_row, n_h2, LANES), F32),
        a1=state(),
        b1=state(),
        z1=state(),
        w1=state(),
        a2=state_two(),
        b2=state_two(),
        z2=state_two(),
        w2=state_two(),
        send_d=each(lambda v: (v, LANES), rows_d),
        got_d=each(lambda v: (n_col, v, LANES), rows_d),
        send_z=each(lambda v: (v, LANES), rows_z),
        got_z=each(lambda v: (n_row, v, LANES), rows_z),
        send_h1=each(lambda v: (v, LANES), rows_h),
        got_h1=each(lambda v: (n_row, 2, v, LANES), rows_h),
        send_h2=each(lambda v: (2, v, LANES), rows_h),
        got_h2=each(lambda v: (n_col, v, LANES), rows_h),
        load_sem=dma((4,)),
        two_sem=dma((n_h2, 2)),
        small_sem=dma((11,)),
        g_out=dma((1,)),
        g_in=dma((1,)),
        d_out=dma((6,)),
        d_in=dma((6,)),
        z_out=dma((6,)),
        z_in=dma((6,)),
        h1_out=dma((6,)),
        h1_in=dma((6,)),
        h2_out=dma((6,)),
        h2_in=dma((6,)),
    )
    scratch, tree = jax.tree.flatten(scratch)

    any_spec = pl.BlockSpec(memory_space=pl.ANY)
    vmem = pl.BlockSpec(memory_space=pltpu.VMEM)
    shapes = [one, two, one, two, (n_d, LANES), (n_h, LANES), (n_z, LANES)]
    held = pl.pallas_call(
        functools.partial(main_kernel, n_row, n_col, 17, 7, tree),
        out_shape=[pltpu.VMEM(shape, F32) for shape in shapes],
        in_specs=[any_spec] * 17,
        out_specs=[vmem] * 7,
        scratch_shapes=scratch,
        compiler_params=pltpu.CompilerParams(
            collective_id=0, has_side_effects=True, vmem_limit_bytes=50 * 1024 * 1024
        ),
    )(
        theta_one,
        theta_two,
        cost_one,
        cost_two,
        packed(depot),
        packed(hub),
        packed(zone),
        mask_one.T,
        mask_two,
        packed(supply),
        packed(demand),
        packed(capacity),
        cot_one,
        cot_two,
        packed(cot_depot),
        packed(cot_hub),
        packed(cot_zone),
    )
    outs = pl.pallas_call(
        write_kernel,
        out_shape=[jax.ShapeDtypeStruct(shape, F32) for shape in shapes],
        in_specs=[vmem] * 7,
        out_specs=[any_spec] * 7,
        scratch_shapes=[dma((19,))],
        compiler_params=pltpu.CompilerParams(vmem_limit_bytes=4 * 1024 * 1024),
    )(*[pltpu.with_memory_space_constraint(v, pltpu.VMEM) for v in held])
    return tuple(outs[:4]) + tuple(v.reshape(-1) for v in outs[4:])


def solution(mesh):
    n_row, n_col = mesh.shape["row"], mesh.shape["col"]
    block, by_row, by_col = P("row", "col"), P("row"), P("col")
    return jax.shard_map(
        functools.partial(on_device, n_row, n_col),
        mesh=mesh,
        in_specs=(
            (block,) * 4 + (by_row, P(), by_col, block, block, by_row, by_col, P(), block, block)
            + (by_row, P(), by_col)
        ),
        out_specs=(block,) * 4 + (by_row, P(), by_col),
        check_vma=False,
    )
```

```python
import functools
import types

import jax
import jax.numpy as jnp
from jax import lax
from jax.experimental import pallas as pl
from jax.experimental.pallas import tpu as pltpu
from jax.sharding import PartitionSpec as P

DEP = 8192
HUB = 4096
LANES = 128
STEP = 0.5
HUB_RATE = 4.0
CHUNK = 32
WIDE = 16
MESH = pl.DeviceIdType.MESH
F32 = jnp.float32
FIRST, SECOND, LINEAR, THIRD, FINAL_HUB, FOURTH = range(6)


def fold(values):
    return jnp.sum(values.reshape(values.shape[0] // 8, 8, LANES), axis=0)


def spread(row):
    return jnp.transpose(jnp.broadcast_to(row, (LANES, LANES)))


def loop(count, body):
    def step(k, carry):
        body(k)
        return carry

    lax.fori_loop(0, count, step, 0)


def arrived(ref, sem):
    pltpu.make_async_copy(ref, ref, sem).wait()


def main_kernel(n_row, n_col, n_in, n_out, tree, *refs):
    (theta_one, theta_two, cost_one, cost_two, depot_hbm, hub_hbm, zone_hbm, mask_one_hbm, mask_two_hbm) = refs[:9]
    (supply_hbm, demand_hbm, capacity_hbm, cot_one, cot_two) = refs[9:14]
    (cot_depot_hbm, cot_hub_hbm, cot_zone_hbm) = refs[14:17]
    (grad_one, grad_two, grad_cost_one, grad_cost_two, grad_depot, grad_hub, grad_zone) = refs[n_in : n_in + n_out]
    m = types.SimpleNamespace(**jax.tree.unflatten(tree, refs[n_in + n_out :]))

    r = lax.axis_index("row")
    c = lax.axis_index("col")
    other = c // 2
    n_d = m.depot.shape[0]
    n_z = m.zone.shape[0]
    n_h1 = theta_one.shape[1] // LANES
    n_h2 = theta_two.shape[0] // LANES
    halves = LANES // CHUNK

    def load(src, dst, sem):
        copy = pltpu.make_async_copy(src, dst, sem)
        copy.start()
        return copy

    mask_one, mask_two = m.mask_one, m.mask_two
    pairs = (
        (depot_hbm, m.depot),
        (capacity_hbm, m.capacity),
        (hub_hbm, m.hub),
        (zone_hbm, m.zone),
        (mask_one_hbm, mask_one),
        (mask_two_hbm, mask_two),
    )
    smalls = [load(src, dst, m.small_sem.at[n]) for n, (src, dst) in enumerate(pairs)]
    loads_one = [load(theta_one, m.th1, m.load_sem.at[0]), load(cost_one, m.co1, m.load_sem.at[1])]

    def load_two(i):
        rows = pl.ds(i * LANES, LANES)
        pairs = ((theta_two, m.th2), (cost_two, m.co2))
        return [load(src.at[rows], dst.at[rows], m.two_sem.at[i, n]) for n, (src, dst) in enumerate(pairs)]

    early = n_h2 // 2
    loads_two = [load_two(i) for i in range(early)]

    barrier = pltpu.get_barrier_semaphore()

    def signal(rr, cc):
        pl.semaphore_signal(barrier, inc=1, device_id=(rr, cc), device_id_type=MESH)

    @pl.when(r != other)
    def _():
        loop(n_col, lambda k: signal(other, lax.rem(c + k, n_col)))
        for q in range(2):
            loop(n_row, lambda k: signal(lax.rem(r + k, n_row), 2 * r + q))

    @pl.when(r == other)
    def _():
        loop(n_col - 1, lambda k: signal(r, lax.rem(c + k + 1, n_col)))
        loop(n_row - 1, lambda k: signal(lax.rem(r + k + 1, n_row), c))
        loop(n_row, lambda k: signal(lax.rem(r + k, n_row), c + 1 - 2 * lax.rem(c, 2)))

    loop(n_col - 1, lambda k: signal(r, lax.rem(c + k + 1, n_col)))
    loop(n_row - 1, lambda k: signal(lax.rem(r + k + 1, n_row), c))

    for copy in smalls:
        copy.wait()

    def hub_one(ref):
        return jnp.concatenate([ref[pl.ds(c * n_h1 + j, 1), :] for j in range(n_h1)], axis=0)

    def hub_two(ref):
        return jnp.concatenate([ref[pl.ds(r * n_h2 + i, 1), :] for i in range(n_h2)], axis=0)

    def set_side(ref, packed):
        for i in range(packed.shape[0]):
            ref[i * LANES : (i + 1) * LANES, :] = spread(packed[i : i + 1])

    level_one = hub_one(m.capacity).astype(F32)
    set_side(m.side_cap, 0.25 * hub_two(m.capacity).astype(F32))

    def sweep_one(body, n_rows, n_cols):
        def block(i, cols):
            cols = list(cols)
            writes = []
            totals = []
            for s in range(halves):
                rows = pl.ds(pl.multiple_of(i * LANES + s * CHUNK, CHUNK), CHUNK)
                total = [None] * n_rows
                for j in range(n_h1):
                    keep = mask_one[j, i].astype(F32) * level_one[j : j + 1]
                    lanes = pl.ds(j * LANES, LANES)
                    by_row, by_col, stores = body(rows, lanes, keep, j)
                    for n, value in enumerate(by_row):
                        total[n] = value if total[n] is None else total[n] + value
                    for n, value in enumerate(by_col):
                        cols[n * n_h1 + j] = cols[n * n_h1 + j] + fold(value)
                    writes += [(ref, rows, lanes, value) for ref, value in stores]
                totals.append((rows, total))
            for ref, rows, lanes, value in writes:
                ref[rows, lanes] = value
            for rows, total in totals:
                for n in range(n_rows):
                    m.stage_depot[n, rows, :] = total[n]
            return tuple(cols)

        zero = jnp.zeros((8, LANES), F32)
        cols = lax.fori_loop(0, n_d, block, (zero,) * (n_h1 * n_cols))
        cols = [jnp.sum(v, axis=0, keepdims=True) for v in cols]
        return [jnp.concatenate(cols[n * n_h1 : (n + 1) * n_h1], axis=0) for n in range(n_cols)]

    def sweep_two(body, n_rows, n_cols, before=None):
        for n in range(n_cols):
            m.stage_zone[n] = jnp.zeros(m.stage_zone.shape[1:], F32)

        def block(n, i):
            rows = pl.ds(pl.multiple_of(n * CHUNK, CHUNK), CHUNK)
            cap = m.side_cap[rows, :]

            def inner(jj, totals):
                totals = list(totals)
                writes = []
                for q in range(WIDE):
                    j = jj * WIDE + q
                    lanes = pl.ds(pl.multiple_of(j * LANES, LANES), LANES)
                    keep = mask_two[i, j].astype(F32) * cap
                    by_row, by_col, stores = body(rows, lanes, keep, j)
                    for k, value in enumerate(by_row):
                        totals[k] = totals[k] + value
                    writes += [(m.stage_zone, (k, j), fold(value)) for k, value in enumerate(by_col)]
                    writes += [(ref, (rows, lanes), value) for ref, value in stores]
                for ref, where, value in writes:
                    if ref is m.stage_zone:
                        value = ref[where] + value
                    ref[where] = value
                return tuple(totals)

            zero = jnp.zeros((CHUNK, LANES), F32)
            totals = lax.fori_loop(0, n_z // WIDE, inner, (zero,) * n_rows)
            for k in range(n_rows):
                m.stage_hub[k, rows, :] = totals[k]

        if before is None:
            loop(n_h2 * halves, lambda n: block(n, n // halves))
        else:
            for i in range(n_h2):
                before(i)
                loop(halves, lambda s: block(i * halves + s, i))

    def packed_rows(stage, n, count):
        parts = [
            jnp.sum(jnp.transpose(stage[n, i * LANES : (i + 1) * LANES, :]), axis=0, keepdims=True)
            for i in range(count)
        ]
        return jnp.concatenate(parts, axis=0)

    def depot_rows(n):
        return packed_rows(m.stage_depot, n, n_d)

    def hub_rows(n):
        return packed_rows(m.stage_hub, n, n_h2)

    def zone_cols(n):
        return jnp.sum(m.stage_zone[n], axis=1)

    def fill(ref, *parts):
        start = 0
        for part in parts:
            ref[start : start + part.shape[0], :] = part
            start += part.shape[0]

    def put(src, dst, out_sem, in_sem, rr, cc):
        pltpu.make_async_remote_copy(
            src_ref=src,
            dst_ref=dst,
            send_sem=out_sem,
            recv_sem=in_sem,
            device_id=(rr, cc),
            device_id_type=MESH,
        ).start()

    def share_cols(t):
        src, got = m.send_d[t], m.got_d[t]
        sems = m.d_out.at[t], m.d_in.at[t]
        loop(n_col - 1, lambda k: put(src, got.at[c], *sems, r, lax.rem(c + k + 1, n_col)))
        got[c] = src[...]

    def share_rows(t):
        src, got = m.send_z[t], m.got_z[t]
        sems = m.z_out.at[t], m.z_in.at[t]
        loop(n_row - 1, lambda k: put(src, got.at[r], *sems, lax.rem(r + k + 1, n_row), c))
        got[r] = src[...]

    def share_one(t):
        sems = m.h1_out.at[t], m.h1_in.at[t]

        @pl.when(r != other)
        def _():
            loop(
                n_col,
                lambda k: put(
                    m.send_h1[t],
                    m.got_h1[t].at[r, lax.rem(c, 2)],
                    *sems,
                    other,
                    lax.rem(c + k, n_col),
                ),
            )

    def share_two(t):
        sems = m.h2_out.at[t], m.h2_in.at[t]
        for q in range(2):

            @pl.when(2 * r + q != c)
            def _():
                loop(
                    n_row,
                    lambda k: put(
                        m.send_h2[t].at[q], m.got_h2[t].at[c], *sems, lax.rem(r + k, n_row), 2 * r + q
                    ),
                )

    def from_cols(t):
        got = m.got_d[t]
        arrived(got.at[pl.ds(0, n_col - 1)], m.d_in.at[t])
        return jnp.sum(got[...], axis=0)

    def from_rows(t):
        got = m.got_z[t]
        arrived(got.at[pl.ds(0, n_row - 1)], m.z_in.at[t])
        return jnp.sum(got[...], axis=0)

    def send_hubs(t, one, two, lead_d, lead_z):
        fill(m.send_h1[t], one)
        for q in range(2):
            m.send_h2[t][q] = two[q * n_h1 : (q + 1) * n_h1]
        fill(m.send_d[t], *lead_d, two, one)
        fill(m.send_z[t], *lead_z, one, two)

    def receive_one(t, start):
        got = m.got_h1[t]
        size = got.shape[2]
        arrived(got.at[pl.ds(0, n_row - 1)], m.h1_in.at[t])
        for q in range(2):
            got[r, q] = m.got_d[t][2 * r + q, start : start + size]
        return jnp.sum(got[...], axis=0)

    def receive_two(t, start):
        got = m.got_h2[t]
        arrived(got.at[pl.ds(0, n_col - 1)], m.h2_in.at[t])
        for q in range(2):

            @pl.when(lax.rem(c, 2) == q)
            def _():
                got[c] = m.got_z[t][other, start + q * n_h1 : start + (q + 1) * n_h1]

        return jnp.sum(got[...], axis=0)

    def receive_hubs(t, all_d, all_z, lead_d, lead_z):
        ones = receive_one(t, lead_d + n_h2)
        one_here = all_z[lead_z : lead_z + n_h1] - receive_two(t, lead_z + n_h1)
        ones = jnp.concatenate([ones[0], ones[1]], axis=0)
        return one_here, ones - all_d[lead_d : lead_d + n_h2]

    hub_a = hub_one(m.hub)
    hub_b = hub_two(m.hub)
    depot_old = m.depot[...]
    zone_old = m.zone[...]
    set_side(m.side_depot, 0.25 * depot_old)
    set_side(m.side_hub, 0.25 * hub_b)
    m.lane_zone[0] = 0.25 * zone_old
    lane_one = 0.25 * hub_a

    def first(th, co, a, b, z, sign, weights):
        def body(rows, lanes, keep, j):
            old = 0.5 * th[rows, lanes].astype(F32)
            cost = 0.25 * co[rows, lanes].astype(F32)
            new = old - cost + sign * weights(rows, j)
            t_old = jnp.tanh(old)
            t_new = jnp.tanh(new)
            value = keep * (0.5 + t_new - 0.5 * t_old)
            return [value], [value], [(a, new - cost), (b, t_new), (z, t_old)]

        return body

    for copy in loads_one:
        copy.wait()
    loads_two += [load_two(i) for i in range(early, n_h2)]
    (one,) = sweep_one(
        first(
            m.th1,
            m.co1,
            m.a1,
            m.b1,
            m.z1,
            -1.0,
            lambda rows, j: m.side_depot[rows, :] + lane_one[j : j + 1],
        ),
        1,
        1,
    )

    def zone_lane(k, j):
        return m.lane_zone[k, pl.ds(j, 1), :]

    def wait_two(i):
        for copy in loads_two[i]:
            copy.wait()

    sweep_two(
        first(
            m.th2,
            m.co2,
            m.a2,
            m.b2,
            m.z2,
            1.0,
            lambda rows, j: m.side_hub[rows, :] + zone_lane(0, j),
        ),
        1,
        1,
        wait_two,
    )
    pairs = (
        (cot_depot_hbm, m.cot_depot),
        (cot_hub_hbm, m.cot_hub),
        (cot_zone_hbm, m.cot_zone),
        (supply_hbm, m.supply),
        (demand_hbm, m.demand),
    )
    smalls = [load(src, dst, m.small_sem.at[n + 6]) for n, (src, dst) in enumerate(pairs)]
    late = [load(cot_one, m.ct1, m.load_sem.at[2]), load(cot_two, m.ct2, m.load_sem.at[3])]
    send_hubs(FIRST, one, hub_rows(0), [depot_rows(0)], [zone_cols(0)])
    pl.semaphore_wait(barrier, n_col * 2 + n_row * 3 - 2 - jnp.where(r == other, 2, 0))
    share_one(FIRST)
    share_two(FIRST)
    share_cols(FIRST)
    share_rows(FIRST)

    for copy in smalls:
        copy.wait()
    adj_depot = m.cot_depot[...]
    adj_zone = m.cot_zone[...]
    adj_a = hub_one(m.cot_hub)
    adj_b = hub_two(m.cot_hub)
    push_a = adj_a * (HUB_RATE / DEP)
    push_b = adj_b * (-HUB_RATE / DEP)
    set_side(m.side_push, push_b)
    supply_level = 0.5 * m.supply[...].astype(F32)
    demand_level = 0.125 * m.demand[...].astype(F32)

    def slopes(b, z, keep, rows, lanes):
        t_new = b[rows, lanes]
        t_old = z[rows, lanes]
        quarter = 0.25 * keep
        square = t_new * t_new
        rest = 1.0 - square
        slope = quarter * rest
        return keep * (0.5 - 0.5 * t_new), slope, quarter * (rest - square + t_old * t_old)

    def window_one(rows, lanes, keep, j):
        past, slope, mixed = slopes(m.b1, m.z1, keep, rows, lanes)
        return [past, slope, slope * push_a[j : j + 1]], [slope], [(m.b1, slope), (m.z1, mixed)]

    def window_two(rows, lanes, keep, j):
        past, slope, mixed = slopes(m.b2, m.z2, keep, rows, lanes)
        return [slope], [past, slope, slope * m.side_push[rows, :]], [(m.b2, slope), (m.z2, mixed)]

    (slope_a,) = sweep_one(window_one, 3, 1)
    past_depot, slope_depot, pushed_depot = depot_rows(0), depot_rows(1), depot_rows(2)
    sweep_two(window_two, 1, 3)
    past_zone, slope_zone, pushed_zone = zone_cols(0), zone_cols(1), zone_cols(2)
    slope_b = hub_rows(0)

    all_d = from_cols(FIRST)
    all_z = from_rows(FIRST)
    one_here, two_here = receive_hubs(FIRST, all_d, all_z, n_d, n_z)
    grow_depot_0 = jnp.exp(STEP * (all_d[0:n_d] * (1.0 / HUB) - supply_level))
    grow_zone_0 = jnp.exp(STEP * (demand_level - all_z[0:n_z] * (1.0 / HUB)))
    depot_0 = depot_old * grow_depot_0
    zone_0 = zone_old * grow_zone_0
    hub_a = hub_a + one_here * (HUB_RATE / DEP)
    hub_b = hub_b + two_here * (HUB_RATE / DEP)

    set_side(m.side_depot, 0.25 * depot_0)
    lane_one_next = 0.25 * hub_a

    def second_one(rows, lanes, keep, j):
        t_new = jnp.tanh(m.a1[rows, lanes] - (m.side_depot[rows, :] + lane_one_next[j : j + 1]))
        return [keep * t_new], [], [(m.a1, t_new)]

    def second_two(rows, lanes, keep, j):
        t_new = jnp.tanh(m.a2[rows, lanes] + (m.side_hub[rows, :] + zone_lane(0, j)))
        return [], [keep * t_new], [(m.a2, t_new)]

    sweep_one(second_one, 1, 0)
    fill(m.send_d[1], depot_rows(0) + past_depot)
    share_cols(SECOND)
    set_side(m.side_hub, 0.25 * hub_b)
    m.lane_zone[0] = 0.25 * zone_0
    sweep_two(second_two, 0, 1)
    fill(m.send_z[1], zone_cols(0) + past_zone)
    share_rows(SECOND)

    for copy in late:
        copy.wait()

    def linear_one(rows, lanes, keep, j):
        t_new = m.a1[rows, lanes]
        beta = (0.25 * keep) * (1.0 - t_new * t_new)
        alpha = beta * (m.ct1[rows, lanes].astype(F32) + 2.0 * push_a[j : j + 1])
        return [alpha, beta], [alpha], [(m.a1, beta), (m.w1, alpha)]

    def linear_two(rows, lanes, keep, j):
        t_new = m.a2[rows, lanes]
        beta = (0.25 * keep) * (1.0 - t_new * t_new)
        alpha = beta * (m.ct2[rows, lanes].astype(F32) + 2.0 * m.side_push[rows, :])
        return [alpha], [alpha, beta], [(m.a2, beta), (m.w2, alpha)]

    (alpha_a,) = sweep_one(linear_one, 2, 1)
    alpha_depot, beta_depot = depot_rows(0), depot_rows(1)
    fill(m.send_d[2], alpha_depot, beta_depot)
    share_cols(LINEAR)
    sweep_two(linear_two, 1, 2)
    alpha_zone, beta_zone = zone_cols(0), zone_cols(1)
    fill(m.send_z[2], alpha_zone, beta_zone)
    share_rows(LINEAR)
    alpha_b = hub_rows(0)

    grow_depot_1 = jnp.exp(STEP * (from_cols(SECOND) * (1.0 / HUB) - supply_level))
    grow_zone_1 = jnp.exp(STEP * (demand_level - from_rows(SECOND) * (1.0 / HUB)))

    push_depot = adj_depot * (depot_0 * grow_depot_1) * (STEP / HUB)
    push_zone = -adj_zone * (zone_0 * grow_zone_1) * (STEP / HUB)
    set_side(m.side_depot, 2.0 * push_depot)
    m.lane_zone[0] = 2.0 * push_zone

    def third_one(rows, lanes, keep, j):
        return [], [m.a1[rows, lanes] * m.side_depot[rows, :]], []

    def third_two(rows, lanes, keep, j):
        return [m.a2[rows, lanes] * zone_lane(0, j)], [], []

    (one,) = sweep_one(third_one, 0, 1)
    sweep_two(third_two, 1, 0)
    one = one + alpha_a
    two = hub_rows(0) + alpha_b
    send_hubs(THIRD, one, two, [], [])
    share_one(THIRD)
    share_two(THIRD)
    share_cols(THIRD)
    share_rows(THIRD)

    all_d = from_cols(LINEAR)
    all_z = from_rows(LINEAR)
    adj_depot = adj_depot * grow_depot_1 - STEP * (all_d[0:n_d] + 2.0 * push_depot * all_d[n_d : 2 * n_d])
    adj_zone = adj_zone * grow_zone_1 + STEP * (all_z[0:n_z] + 2.0 * push_zone * all_z[n_z : 2 * n_z])
    last_depot = adj_depot * depot_0 * (STEP / HUB)
    last_zone = -adj_zone * zone_0 * (STEP / HUB)
    set_side(m.side_last, last_depot)
    m.lane_zone[1] = last_zone

    def both_one(rows, lanes, keep, j):
        weight = 2.0 * m.side_last[rows, :] - 0.5 * m.side_depot[rows, :]
        return [], [m.b1[rows, lanes] * weight], []

    def both_two(rows, lanes, keep, j):
        return [m.b2[rows, lanes] * (2.0 * zone_lane(1, j) - 0.5 * zone_lane(0, j))], [], []

    (more,) = sweep_one(both_one, 0, 1)
    one = one + more - push_a * slope_a
    sweep_two(both_two, 1, 0)
    two = two + hub_rows(0) - push_b * slope_b
    fill(m.send_h1[4], one, slope_a)
    fill(m.send_d[4], two, slope_b, one, slope_a)
    share_one(FINAL_HUB)
    share_cols(FINAL_HUB)

    def state(total, weight, last, slope, mixed):
        part = weight * slope
        return total - part + last * mixed, 0.5 * part - total - last * slope

    all_d = from_cols(THIRD)
    all_z = from_rows(THIRD)
    one_here, two_here = receive_hubs(THIRD, all_d, all_z, 0, 0)
    adj_a = adj_a - STEP * one_here
    adj_b = adj_b - STEP * two_here
    last_a = adj_a * (HUB_RATE / DEP)
    last_b = adj_b * (-HUB_RATE / DEP)

    def fourth_one(rows, lanes, keep, j):
        return [m.b1[rows, lanes] * last_a[j : j + 1]], [], []

    def fourth_two(rows, lanes, keep, j):
        return [], [m.b2[rows, lanes] * m.side_hub[rows, :]], []

    def last_sum(alpha, beta, push, slope, pushed, last, value):
        return alpha + 2.0 * push * beta + (2.0 * last - push) * slope - pushed + 2.0 * value

    sweep_one(fourth_one, 1, 0)
    depot_value = depot_rows(0)
    fill(
        m.send_d[5],
        last_sum(alpha_depot, beta_depot, push_depot, slope_depot, pushed_depot, last_depot, depot_value),
    )
    share_cols(FOURTH)
    set_side(m.side_hub, last_b)
    sweep_two(fourth_two, 0, 1)
    zone_value = zone_cols(0)
    fill(
        m.send_z[5],
        last_sum(alpha_zone, beta_zone, push_zone, slope_zone, pushed_zone, last_zone, zone_value),
    )
    share_rows(FOURTH)

    all_d = from_cols(FINAL_HUB)
    ones = receive_one(FINAL_HUB, 2 * n_h2)
    sums = jnp.concatenate([ones[0, 0:n_h1], ones[1, 0:n_h1]], axis=0)
    sums_slope = jnp.concatenate([ones[0, n_h1 : 2 * n_h1], ones[1, n_h1 : 2 * n_h1]], axis=0)
    sums = sums - 2.0 * last_b * sums_slope
    two_sum = all_d[0:n_h2] + 2.0 * last_b * all_d[n_h2 : 2 * n_h2]
    got_g = m.got_g
    got_g[r] = adj_b + STEP * (two_sum - sums)
    sems = m.g_out.at[0], m.g_in.at[0]
    loop(n_row - 1, lambda k: put(got_g.at[r], got_g.at[r], *sems, lax.rem(r + k + 1, n_row), c))

    def end_one(rows, lanes, keep, j):
        twice = m.side_depot[rows, :]
        total = m.w1[rows, lanes] + twice * m.a1[rows, lanes]
        weight = 0.5 * twice + push_a[j : j + 1]
        last = m.side_last[rows, :] + last_a[j : j + 1]
        theta, cost = state(total, weight, last, m.b1[rows, lanes], m.z1[rows, lanes])
        return [], [], [(grad_one, theta), (grad_cost_one, cost)]

    def end_two(rows, lanes, keep, j):
        twice = zone_lane(0, j)
        total = m.w2[rows, lanes] + twice * m.a2[rows, lanes]
        weight = 0.5 * twice + m.side_push[rows, :]
        last = zone_lane(1, j) + m.side_hub[rows, :]
        theta, cost = state(total, weight, last, m.b2[rows, lanes], m.z2[rows, lanes])
        return [], [], [(grad_two, theta), (grad_cost_two, cost)]

    sweep_one(end_one, 0, 0)
    sweep_two(end_two, 0, 0)

    grad_depot[...] = adj_depot * grow_depot_0 - STEP * from_cols(FOURTH)
    grad_zone[...] = adj_zone * grow_zone_0 + STEP * from_rows(FOURTH)
    arrived(got_g.at[pl.ds(0, n_row - 1)], m.g_in.at[0])
    for k in range(n_row):
        grad_hub[k * n_h2 : (k + 1) * n_h2, :] = got_g[k]

    arrived(got_g.at[pl.ds(0, n_row - 1)], m.g_out.at[0])
    for t in range(6):
        arrived(m.got_d[t].at[pl.ds(0, n_col - 1)], m.d_out.at[t])
        if t != FINAL_HUB:
            arrived(m.got_z[t].at[pl.ds(0, n_row - 1)], m.z_out.at[t])
        if t in (FIRST, THIRD, FINAL_HUB):

            @pl.when(r != other)
            def _():
                arrived(m.got_h1[t], m.h1_out.at[t])

        if t in (FIRST, THIRD):
            arrived(m.got_h2[t].at[pl.ds(0, n_row)], m.h2_out.at[t])

            @pl.when(r != other)
            def _():
                arrived(m.got_h2[t].at[pl.ds(0, n_row)], m.h2_out.at[t])


def write_kernel(*refs):
    count = (len(refs) - 1) // 2
    sem = refs[-1]
    copies = []
    for src, dst in zip(refs[:count], refs[count:-1]):
        rows = src.shape[0]
        parts = 4 if rows >= 512 else 1
        for n in range(parts):
            piece = pl.ds(n * (rows // parts), rows // parts)
            copies.append(pltpu.make_async_copy(src.at[piece], dst.at[piece], sem.at[len(copies)]))
    for copy in copies:
        copy.start()
    for copy in copies:
        copy.wait()


def on_device(n_row, n_col, *args):
    (theta_one, theta_two, cost_one, cost_two, depot, hub, zone, mask_one, mask_two) = args[:9]
    (supply, demand, capacity, cot_one, cot_two, cot_depot, cot_hub, cot_zone) = args[9:]

    def packed(vector):
        return vector.reshape(vector.shape[0] // LANES, LANES)

    depots, hubs_one = theta_one.shape
    hubs_two, zones = theta_two.shape
    n_d, n_z, n_h = depots // LANES, zones // LANES, hub.shape[0] // LANES
    n_h1, n_h2 = hubs_one // LANES, hubs_two // LANES
    one, two = (depots, hubs_one), (hubs_two, zones)

    def rounded(rows):
        return -(-rows // 8) * 8

    def vec(rows, dtype=F32):
        return pltpu.VMEM((rows, LANES), dtype)

    dma = pltpu.SemaphoreType.DMA
    bf16 = jnp.bfloat16
    hubs = n_h1 + n_h2
    rows_d = [rounded(v) for v in (n_d + hubs, n_d, 2 * n_d, hubs, 2 * hubs, n_d)]
    rows_z = [rounded(v) for v in (n_z + hubs, n_z, 2 * n_z, hubs, 8, n_z)]
    rows_h = [n_h1, 0, 0, n_h1, 2 * n_h1, 0]

    def state():
        return pltpu.VMEM(one, F32)

    def state_two():
        return pltpu.VMEM(two, F32)

    def each(shape_of, rows):
        return [pltpu.VMEM(shape_of(v), F32) if v else None for v in rows]

    scratch = dict(
        th1=pltpu.VMEM(one, bf16),
        th2=pltpu.VMEM(two, bf16),
        co1=pltpu.VMEM(one, bf16),
        co2=pltpu.VMEM(two, bf16),
        ct1=pltpu.VMEM(one, bf16),
        ct2=pltpu.VMEM(two, bf16),
        mask_one=pltpu.SMEM((n_h1, n_d), jnp.int32),
        mask_two=pltpu.SMEM((n_h2, n_z), jnp.int32),
        depot=vec(n_d),
        hub=vec(n_h),
        zone=vec(n_z),
        supply=vec(n_d, jnp.int32),
        demand=vec(n_z, jnp.int32),
        capacity=vec(n_h, jnp.int32),
        cot_depot=vec(n_d),
        cot_hub=vec(n_h),
        cot_zone=vec(n_z),
        side_depot=vec(depots),
        side_last=vec(depots),
        side_hub=vec(hubs_two),
        side_push=vec(hubs_two),
        side_cap=vec(hubs_two),
        lane_zone=pltpu.VMEM((2, n_z, LANES), F32),
        stage_depot=pltpu.VMEM((3, depots, LANES), F32),
        stage_hub=pltpu.VMEM((1, hubs_two, LANES), F32),
        stage_zone=pltpu.VMEM((3, n_z, 8, LANES), F32),
        got_g=pltpu.VMEM((n_row, n_h2, LANES), F32),
        a1=state(),
        b1=state(),
        z1=state(),
        w1=state(),
        a2=state_two(),
        b2=state_two(),
        z2=state_two(),
        w2=state_two(),
        send_d=each(lambda v: (v, LANES), rows_d),
        got_d=each(lambda v: (n_col, v, LANES), rows_d),
        send_z=each(lambda v: (v, LANES), rows_z),
        got_z=each(lambda v: (n_row, v, LANES), rows_z),
        send_h1=each(lambda v: (v, LANES), rows_h),
        got_h1=each(lambda v: (n_row, 2, v, LANES), rows_h),
        send_h2=each(lambda v: (2, v, LANES), rows_h),
        got_h2=each(lambda v: (n_col, v, LANES), rows_h),
        load_sem=dma((4,)),
        two_sem=dma((n_h2, 2)),
        small_sem=dma((11,)),
        g_out=dma((1,)),
        g_in=dma((1,)),
        d_out=dma((6,)),
        d_in=dma((6,)),
        z_out=dma((6,)),
        z_in=dma((6,)),
        h1_out=dma((6,)),
        h1_in=dma((6,)),
        h2_out=dma((6,)),
        h2_in=dma((6,)),
    )
    scratch, tree = jax.tree.flatten(scratch)

    any_spec = pl.BlockSpec(memory_space=pl.ANY)
    vmem = pl.BlockSpec(memory_space=pltpu.VMEM)
    shapes = [one, two, one, two, (n_d, LANES), (n_h, LANES), (n_z, LANES)]
    held = pl.pallas_call(
        functools.partial(main_kernel, n_row, n_col, 17, 7, tree),
        out_shape=[pltpu.VMEM(shape, F32) for shape in shapes],
        in_specs=[any_spec] * 17,
        out_specs=[vmem] * 7,
        scratch_shapes=scratch,
        compiler_params=pltpu.CompilerParams(
            collective_id=0, has_side_effects=True, vmem_limit_bytes=50 * 1024 * 1024
        ),
    )(
        theta_one,
        theta_two,
        cost_one,
        cost_two,
        packed(depot),
        packed(hub),
        packed(zone),
        mask_one.T,
        mask_two,
        packed(supply),
        packed(demand),
        packed(capacity),
        cot_one,
        cot_two,
        packed(cot_depot),
        packed(cot_hub),
        packed(cot_zone),
    )
    outs = pl.pallas_call(
        write_kernel,
        out_shape=[jax.ShapeDtypeStruct(shape, F32) for shape in shapes],
        in_specs=[vmem] * 7,
        out_specs=[any_spec] * 7,
        scratch_shapes=[dma((19,))],
        compiler_params=pltpu.CompilerParams(vmem_limit_bytes=4 * 1024 * 1024),
    )(*[pltpu.with_memory_space_constraint(v, pltpu.VMEM) for v in held])
    return tuple(outs[:4]) + tuple(v.reshape(-1) for v in outs[4:])


def solution(mesh):
    n_row, n_col = mesh.shape["row"], mesh.shape["col"]
    block, by_row, by_col = P("row", "col"), P("row"), P("col")
    return jax.shard_map(
        functools.partial(on_device, n_row, n_col),
        mesh=mesh,
        in_specs=(
            (block,) * 4 + (by_row, P(), by_col, block, block, by_row, by_col, P(), block, block)
            + (by_row, P(), by_col)
        ),
        out_specs=(block,) * 4 + (by_row, P(), by_col),
        check_vma=False,
    )
```
